32 devices in a mesh: expert: 8 (over z, x), tensor: 4 (over y, core).
Axes of the slice: x: 2, y: 2, z: 4, core: 2. Of those that a mesh axis runs over, the one named last changes fastest.
Arguments:
- tokens: bfloat16 [9456, 512], P('expert'), may hold values from -46 to 46
- qkv_weight: bfloat16 [3, 512, 512], P(None, None, 'tensor'), may hold values from -0.25 to 0.25
- out_weight: bfloat16 [512, 512], P('tensor'), may hold values from -2 to 2
- gain_attn: float32 [512], replicated, may hold values from 0.5 to 1.5
- gain_moe: float32 [512], replicated, may hold values from 0.5 to 1.5
- router_weight: bfloat16 [512, 4], replicated, may hold values from -0.1875 to 0.1875
- expert_in: bfloat16 [8, 512, 1024], P('expert', None, 'tensor'), may hold values from -0.25 to 0.25
- expert_out: bfloat16 [8, 1024, 512], P('expert', 'tensor'), may hold values from -0.25 to 0.25
- expert_ids: int32 [9456, 2], P('expert'), may hold values from 0 to 3, all different within a row
- priority: int32 [8, 1182], P('expert'), may hold values from 0 to 1181, each once within a row
- cotangent: bfloat16 [9456, 512], P('expert'), may hold values from -6 to 6
Outputs:
- result: bfloat16 [9456, 512], P('expert')
- grad_tokens: float32 [9456, 512], P('expert')
- grad_qkv: float32 [3, 512, 512], P(None, None, 'tensor')
- grad_out_weight: float32 [512, 512], P('tensor')
- grad_gain_attn: float32 [512], replicated
- grad_gain_moe: float32 [512], replicated
- grad_router: float32 [512, 4], replicated
- grad_expert_in: float32 [8, 512, 1024], P('expert', None, 'tensor')
- grad_expert_out: float32 [8, 1024, 512], P('expert', 'tensor')
- stats: float32 [3], replicated
The draws below stay inside these ranges and needn't reach their ends.
Inputs may be any that keep to these rules, and one draw needn't show every extreme that they name: `expert_ids`: each token names two different experts; every expert is named by some token. `priority`: each row holds every place 0 to 1181 once; place 0 goes first.
All inputs are finite; a program needn't handle non-finite values.
Results may differ from the reference program's by a relative error of at most 0.013.
The reference program's roundings to bfloat16 on the way count: a program that leaves them out, or rounds other values in their place, can miss the bound.
Values may be sent and summed in bfloat16 or wider, within the bound.
No kernel may reach another device: no remote copies, remote signals or barrier semaphores. Data moves between devices by JAX's collectives and lax.ppermute only.
A program may use at most 192 MiB of HBM per device.

```python
import math
import jax
import jax.numpy as jnp
from jax import lax

D = 512
HEADS = 8
HD = 64
FF = 2048
LEN = 197
ROWS = 1182
EXPERTS = 4
CAP = 738
TOKENS = 9456
N_EXPERT = 8


def draw_tokens(key, part):
    keyone, keytwo, keythree = jax.random.split(key, 3)
    position = jnp.arange(TOKENS, dtype=jnp.float32) / TOKENS
    rising = jnp.exp(math.log(3.0) * position)[:, None]
    columns = jnp.exp(jax.random.uniform(keythree, (1, D), jnp.float32, math.log(0.7), math.log(1.4)))
    base = jnp.clip(jax.random.normal(keyone, (TOKENS, D), jnp.float32), -6.0, 6.0)
    spread = jnp.exp(jax.random.uniform(keytwo, (TOKENS, 1), jnp.float32, math.log(0.6), math.log(1.8)))
    return (base * spread * columns * rising).astype(jnp.bfloat16)


def shard_levels(stream_key, shape, cuts, low, largest):
    def one(dim, parts):
        heights = jax.random.uniform(jax.random.fold_in(jax.random.fold_in(stream_key, 6), dim), (parts,), jnp.float32, low / len(cuts), largest / len(cuts))
        return jnp.repeat(jnp.exp(heights), shape[dim] // parts).reshape((-1,) + (1,) * (len(shape) - dim - 1))

    level = one(*cuts[0])
    for cut in cuts[1:]:
        level = level * one(*cut)
    return level


def choose_distinct(rng, rows, count, top, lift):
    order = jax.random.permutation(jax.random.fold_in(rng, 1), count)
    pull = order
    for power in range(3):
        pull = pull * pull // count
    pull = pull * lift // count
    tickets = jax.random.randint(jax.random.fold_in(rng, 2), (rows, count), 0, 4096) + pull
    fixed_rows = jax.random.permutation(jax.random.fold_in(rng, 3), rows)[jnp.arange(count) % rows]
    tickets = jnp.where(jnp.arange(rows)[:, None] == fixed_rows[None, :], 1 << 14, tickets)
    score = tickets * count + jnp.arange(count)
    return lax.top_k(score.astype(jnp.int32), top)[1].astype(jnp.int32)


def scatter_about(key, dims, scale, most, cuts=(), held_as=jnp.bfloat16):
    level = shard_levels(key, dims, cuts, -0.22, 0.18) if cuts else 1.0
    drawn = jax.random.normal(key, dims, jnp.float32) * scale * level
    return jnp.minimum(jnp.maximum(drawn, -most), most).astype(held_as)


def setup_inputs(seed: int = 0) -> dict:
    key_of = jax.random.split(jax.random.key(seed), 12)
    return {
        "tokens": draw_tokens(jax.random.fold_in(key_of[11], 71), 0),
        "qkv_weight": scatter_about(key_of[1], (3, D, D), D ** -0.5, 0.25, ((2, 4),)),
        "out_weight": scatter_about(key_of[2], (D, D), (D // 64) ** -0.5, 2.0, ((0, 4),)),
        "gain_attn": jnp.clip(1.0 + 0.1 * jax.random.normal(key_of[3], (D,), jnp.float32), 0.5, 1.5),
        "gain_moe": jnp.clip(1.0 + 0.1 * jax.random.normal(key_of[4], (D,), jnp.float32), 0.5, 1.5),
        "router_weight": scatter_about(key_of[5], (D, EXPERTS), (2 * D) ** -0.5, 0.1875),
        "expert_in": scatter_about(key_of[6], (2 * EXPERTS, D, FF // 2), D ** -0.5, 0.25, ((0, 8), (2, 4))),
        "expert_out": scatter_about(key_of[7], (2 * EXPERTS, FF // 2, D), (FF // 4) ** -0.5, 0.25, ((0, 8), (1, 4))),
        "expert_ids": choose_distinct(key_of[8], TOKENS, EXPERTS, 2, 4096),
        "priority": jax.vmap(lambda own: jax.random.permutation(own, ROWS))(jax.random.split(key_of[9], N_EXPERT)).reshape((N_EXPERT, ROWS)).astype(jnp.int32),
        "cotangent": scatter_about(key_of[10], (TOKENS, D), 1.0, 6.0, ((0, 8),)),
    }


EPSILON = 1e-06
HIGHEST = lax.Precision.HIGHEST

@jax.custom_vjp
def low(v):
    return lax.optimization_barrier(v.astype(jnp.bfloat16)).astype(jnp.float32)

@jax.custom_vjp
def low_back(v):
    return v

def low_keep(v):
    return (low(v), None)

def low_pass(kept, grad):
    return (grad,)

def back_keep(v):
    return (v, None)

def back_low(kept, grad):
    return (low(grad),)
low.defvjp(low_keep, low_pass)
low_back.defvjp(back_keep, back_low)

def rms_norm(values, gain):
    return values * lax.rsqrt(lax.optimization_barrier(jnp.mean(values * values, axis=-1, keepdims=True)) + EPSILON) * gain

def slot_table(expert_ids, ranking):
    count = expert_ids.shape[0]
    ordering = jnp.zeros((count,), jnp.int32).at[ranking].set(jnp.arange(count, dtype=jnp.int32))
    expert_iota = jnp.arange(EXPERTS, dtype=jnp.int32)
    leading = (expert_ids[:, 0:1] == expert_iota[None, :]).astype(jnp.int32)
    trailing = (expert_ids[:, 1:2] == expert_iota[None, :]).astype(jnp.int32)
    lead_sorted = leading[ordering]
    trail_sorted = trailing[ordering]
    lead_before = (jnp.cumsum(lead_sorted, axis=0) - lead_sorted)[ranking]
    trail_before = (jnp.cumsum(trail_sorted, axis=0) - trail_sorted)[ranking] + lax.optimization_barrier(jnp.sum(leading, axis=0))[None, :]
    lead_place = lax.optimization_barrier(jnp.sum(lead_before * leading, axis=1))
    trail_place = lax.optimization_barrier(jnp.sum(trail_before * trailing, axis=1))
    placing = jnp.stack([lead_place, trail_place], axis=1).astype(jnp.int32)
    return jnp.where(placing < CAP, expert_ids * CAP + placing, EXPERTS * CAP).astype(jnp.int32)

def attend(block, qkv_w, out_w, gain):
    groups = block.shape[0] // LEN
    normed = low(rms_norm(block, gain))
    qkv = low_back(low(jnp.einsum('td,sdf->stf', normed, qkv_w, precision=HIGHEST)))
    shaped = qkv.reshape(3, groups, LEN, HEADS, HD)
    scores = jnp.einsum('gqhe,gkhe->ghqk', shaped[0], shaped[1], precision=HIGHEST) / math.sqrt(HD)
    scores = low_back(scores)
    probs = low(jax.nn.softmax(scores, axis=-1))
    head_rows = jnp.einsum('ghqk,gkhe->gqhe', probs, shaped[2], precision=HIGHEST).reshape(groups * LEN, D)
    head_rows = low_back(low(head_rows))
    return low_back(jnp.dot(head_rows, out_w, precision=HIGHEST))

def expert_ffn(rows_in, w_in, w_out):
    pre_act = low_back(jnp.dot(rows_in, w_in, precision=HIGHEST))
    activated = low(jax.nn.gelu(pre_act, approximate=False))
    return low_back(low(jnp.dot(activated, w_out, precision=HIGHEST)))

def reference(tokens, qkv_weight, out_weight, gain_attn, gain_moe, router_weight, expert_in, expert_out, expert_ids, priority, cotangent):
    slots = jax.vmap(slot_table)(expert_ids.reshape(N_EXPERT, ROWS, 2), priority)
    slot_count = EXPERTS * CAP

    def forward(xs, qkv_w, out_w, gain_one, gain_two, router_w, w_in_halves, w_out_halves):
        w_in = w_in_halves.reshape(EXPERTS, 2, D, FF // 2).transpose(0, 2, 1, 3).reshape(EXPERTS, D, FF)
        w_out = w_out_halves.reshape(EXPERTS, FF, D)
        attn = lax.map(jax.checkpoint(lambda block: attend(block, qkv_w, out_w, gain_one)), xs.reshape(N_EXPERT, ROWS, D)).reshape(TOKENS, D)
        residual = xs + attn
        normed = low(rms_norm(residual, gain_two))
        logits = jnp.dot(normed, router_w, precision=HIGHEST)
        chosen = jnp.take_along_axis(logits, expert_ids, axis=1)
        gates = jax.nn.softmax(chosen, axis=1)

        def place(rows_dev, slot_dev):
            buffer = jnp.zeros((slot_count + 1, D), jnp.float32)
            buffer = buffer.at[slot_dev[:, 0]].add(rows_dev).at[slot_dev[:, 1]].add(rows_dev)
            return buffer[:slot_count]
        dispatched = low_back(jax.vmap(place)(normed.reshape(N_EXPERT, ROWS, D), slots))
        per_expert = dispatched.reshape(N_EXPERT, EXPERTS, CAP, D).transpose(1, 0, 2, 3).reshape(EXPERTS, N_EXPERT * CAP, D)
        outputs = lax.map(jax.checkpoint(lambda element: expert_ffn(element[0], element[1], element[2])), (per_expert, w_in, w_out))
        returned = outputs.reshape(EXPERTS, N_EXPERT, CAP, D).transpose(1, 0, 2, 3).reshape(N_EXPERT, slot_count, D)
        padded = jnp.concatenate([returned, jnp.zeros((N_EXPERT, 1, D), jnp.float32)], axis=1)
        taken = jax.vmap(lambda table_rows, slot_rows: table_rows[slot_rows])(padded, slots)
        moe = lax.optimization_barrier(jnp.sum(gates.reshape(N_EXPERT, ROWS, 2, 1) * taken, axis=2)).reshape(TOKENS, D)
        result = residual + moe
        stats = jnp.stack([jnp.sqrt(jnp.mean(xs * xs)), jnp.sqrt(jnp.mean(attn * attn)), jnp.sqrt(jnp.mean(moe * moe))])
        return (result, stats)
    primals = (tokens.astype(jnp.float32), qkv_weight.astype(jnp.float32), out_weight.astype(jnp.float32), gain_attn.astype(jnp.float32), gain_moe.astype(jnp.float32), router_weight.astype(jnp.float32), expert_in.astype(jnp.float32), expert_out.astype(jnp.float32))
    result, pullback, stats = jax.vjp(forward, *primals, has_aux=True)
    grads = pullback(cotangent.astype(jnp.float32))
    return (result.astype(jnp.bfloat16), grads[0], grads[1], grads[2], grads[3], grads[4], grads[5], grads[6], grads[7], stats)
```

```python
import math

import jax
import jax.numpy as jnp
from jax import lax
from jax.experimental import pallas as pl
from jax.experimental.pallas import tpu as pltpu
from jax.sharding import PartitionSpec as P

HD = 64
LEN = 197


EPSILON = 1e-06
HIGHEST = lax.Precision.HIGHEST


def slot_table(expert_ids, ranking, experts, capacity):
    count = expert_ids.shape[0]
    ordering = jnp.zeros((count,), jnp.int32).at[ranking].set(jnp.arange(count, dtype=jnp.int32))
    expert_iota = jnp.arange(experts, dtype=jnp.int32)
    leading = (expert_ids[:, 0:1] == expert_iota[None, :]).astype(jnp.int32)
    trailing = (expert_ids[:, 1:2] == expert_iota[None, :]).astype(jnp.int32)
    lead_sorted = leading[ordering]
    trail_sorted = trailing[ordering]
    lead_before = (jnp.cumsum(lead_sorted, axis=0) - lead_sorted)[ranking]
    trail_before = (jnp.cumsum(trail_sorted, axis=0) - trail_sorted)[ranking] + jnp.sum(
        leading, axis=0
    )[None, :]
    lead_place = jnp.sum(lead_before * leading, axis=1)
    trail_place = jnp.sum(trail_before * trailing, axis=1)
    placing = jnp.stack([lead_place, trail_place], axis=1)
    return jnp.where(placing < capacity, expert_ids * capacity + placing, experts * capacity)


def norm_parts(values, gain):
    scaling = lax.rsqrt(jnp.mean(values * values, axis=-1, keepdims=True) + EPSILON)
    unit_rows = values * scaling
    return (unit_rows * gain, unit_rows, scaling)


def norm_back(incoming, unit_rows, scaling, gain):
    inner = incoming * gain
    spread_back = scaling * (
        inner - unit_rows * jnp.mean(inner * unit_rows, axis=-1, keepdims=True)
    )
    return (spread_back, jnp.sum(incoming * unit_rows, axis=0))


def pair_tables(slot_block, slot_count):
    slot_iota = jnp.arange(slot_count, dtype=jnp.int32)[None, :]
    return (
        (slot_block[:, 0:1] == slot_iota).astype(jnp.bfloat16),
        (slot_block[:, 1:2] == slot_iota).astype(jnp.bfloat16),
    )


def to_experts(buffer):
    doubled = jnp.repeat(buffer, 2, axis=0)
    moved = lax.all_to_all(doubled, "expert", split_axis=0, concat_axis=0, tiled=True)
    return moved.reshape(moved.shape[0] * moved.shape[1], moved.shape[2])


def tensor_total(summand):
    return lax.psum(summand, "tensor")


def from_experts(rows_back, experts, capacity):
    shaped_back = rows_back.reshape(2 * experts, capacity, rows_back.shape[1])
    moved = lax.all_to_all(shaped_back, "expert", split_axis=0, concat_axis=0, tiled=True)
    width = moved.shape[2]
    halves = jnp.sum(moved.reshape(experts, 2, capacity, width), axis=1)
    return halves.astype(jnp.bfloat16).reshape(experts * capacity, width)


def per_device_slots(
    tokens,
    qkv_weight,
    out_weight,
    gain_attn,
    gain_moe,
    router_weight,
    expert_in,
    expert_out,
    expert_ids,
    priority,
    cotangent,
):
    row_count, features = tokens.shape
    local_width = qkv_weight.shape[2]
    heads_here = local_width // HD
    images = row_count // LEN
    experts = router_weight.shape[1]
    capacity = max(2, 5 * row_count // (2 * experts))
    slot_count = experts * capacity
    block_rows = 2 * LEN
    blocks = row_count // block_rows
    slot_index = slot_table(expert_ids, priority[0], experts, capacity)
    slot_blocks = slot_index.reshape(blocks, block_rows, 2)
    score_root = math.sqrt(HD)
    inputs = tokens.astype(jnp.float32)
    normed_one, unit_one, scale_one = norm_parts(inputs, gain_attn)
    normed_one = normed_one.astype(jnp.bfloat16)
    qkv = jnp.einsum(
        "td,sdf->stf", normed_one, qkv_weight, preferred_element_type=jnp.float32
    ).astype(jnp.bfloat16)
    shaped = qkv.reshape(3, images, LEN, heads_here, HD)
    scores = (
        jnp.einsum("gqhe,gkhe->ghqk", shaped[0], shaped[1], preferred_element_type=jnp.float32)
        / score_root
    )
    row_peak = jnp.max(scores, axis=-1, keepdims=True)
    weights = jnp.exp(scores - row_peak)
    weight_total = jnp.sum(weights, axis=-1, keepdims=True)
    probs = weights / weight_total
    log_total = row_peak + jnp.log(weight_total)
    head_rows = (
        jnp.einsum(
            "ghqk,gkhe->gqhe",
            probs.astype(jnp.bfloat16),
            shaped[2],
            preferred_element_type=jnp.float32,
        )
        .reshape(row_count, local_width)
        .astype(jnp.bfloat16)
    )
    attn = lax.psum(jnp.dot(head_rows, out_weight, preferred_element_type=jnp.float32), "tensor")
    residual = inputs + attn
    normed_two, unit_two, scale_two = norm_parts(residual, gain_moe)
    normed_two = normed_two.astype(jnp.bfloat16)
    logits = jnp.dot(normed_two, router_weight, preferred_element_type=jnp.float32)
    expert_iota = jnp.arange(experts, dtype=jnp.int32)
    choosing = (expert_ids[:, :, None] == expert_iota[None, None, :]).astype(jnp.float32)
    chosen = jnp.sum(choosing * logits[:, None, :], axis=2)
    gates = jax.nn.softmax(chosen, axis=1)

    def collect(carry, element):
        leading, trailing = pair_tables(element[0], slot_count)
        return (
            carry
            + jnp.einsum(
                "tc,td->cd", leading + trailing, element[1], preferred_element_type=jnp.float32
            ),
            None,
        )

    dispatched, ignored = lax.scan(
        collect,
        jnp.zeros((slot_count, features), jnp.float32),
        (slot_blocks, normed_two.reshape(blocks, block_rows, features)),
    )
    dispatched = dispatched.astype(jnp.bfloat16).reshape(experts, capacity, features)
    received = to_experts(dispatched)
    pre_act = jnp.dot(received, expert_in[0], preferred_element_type=jnp.float32)
    activated = jax.nn.gelu(pre_act, approximate=False).astype(jnp.bfloat16)
    returned = from_experts(
        tensor_total(jnp.dot(activated, expert_out[0], preferred_element_type=jnp.float32)),
        experts,
        capacity,
    )
    grad_y = cotangent.astype(jnp.float32)

    def combine(carry, element):
        slot_block, gate_block, grad_block = element
        leading, trailing = pair_tables(slot_block, slot_count)
        got_lead = jnp.dot(leading, returned, preferred_element_type=jnp.float32)
        got_trail = jnp.dot(trailing, returned, preferred_element_type=jnp.float32)
        mixed = gate_block[:, 0:1] * got_lead + gate_block[:, 1:2] * got_trail
        gate_grad = jnp.stack(
            [jnp.sum(grad_block * got_lead, axis=1), jnp.sum(grad_block * got_trail, axis=1)],
            axis=1,
        )
        carry = carry + jnp.einsum(
            "tc,td->cd",
            leading,
            (gate_block[:, 0:1] * grad_block).astype(jnp.bfloat16),
            preferred_element_type=jnp.float32,
        )
        carry = carry + jnp.einsum(
            "tc,td->cd",
            trailing,
            (gate_block[:, 1:2] * grad_block).astype(jnp.bfloat16),
            preferred_element_type=jnp.float32,
        )
        return (carry, (mixed, gate_grad))

    grad_slots, (moe, gate_grad) = lax.scan(
        combine,
        jnp.zeros((slot_count, features), jnp.float32),
        (
            slot_blocks,
            gates.reshape(blocks, block_rows, 2),
            grad_y.reshape(blocks, block_rows, features),
        ),
    )
    moe = moe.reshape(row_count, features)
    gate_grad = gate_grad.reshape(row_count, 2)
    result = (residual + moe).astype(jnp.bfloat16)
    grad_rows = to_experts(grad_slots.astype(jnp.bfloat16).reshape(experts, capacity, features))
    grad_act = jnp.einsum("rd,fd->rf", grad_rows, expert_out[0], preferred_element_type=jnp.float32)
    ignored, gelu_back = jax.vjp(lambda values: jax.nn.gelu(values, approximate=False), pre_act)
    grad_pre = gelu_back(grad_act)[0].astype(jnp.bfloat16)
    grad_expert_out = jnp.einsum(
        "rf,rd->fd", activated, grad_rows, preferred_element_type=jnp.float32
    )
    grad_expert_in = jnp.einsum("rd,rf->df", received, grad_pre, preferred_element_type=jnp.float32)
    grad_sent = from_experts(
        tensor_total(
            jnp.einsum("rf,df->rd", grad_pre, expert_in[0], preferred_element_type=jnp.float32)
        ),
        experts,
        capacity,
    )
    grad_choice = gates * (gate_grad - jnp.sum(gates * gate_grad, axis=1, keepdims=True))
    grad_logits = jnp.sum(choosing * grad_choice[:, :, None], axis=1)
    grad_router = jnp.einsum(
        "td,te->de", normed_two.astype(jnp.float32), grad_logits, precision=HIGHEST
    )
    router_back = jnp.einsum(
        "te,de->td", grad_logits, router_weight.astype(jnp.float32), precision=HIGHEST
    )

    def spread_rows(slot_block):
        leading, trailing = pair_tables(slot_block, slot_count)
        return jnp.dot(leading + trailing, grad_sent, preferred_element_type=jnp.float32)

    grad_normed_two = lax.map(spread_rows, slot_blocks).reshape(row_count, features) + router_back
    residual_back, grad_gain_moe = norm_back(grad_normed_two, unit_two, scale_two, gain_moe)
    grad_residual = grad_y + residual_back
    grad_attn = grad_residual.astype(jnp.bfloat16)
    grad_out_weight = jnp.einsum(
        "tf,td->fd", head_rows, grad_attn, preferred_element_type=jnp.float32
    )
    grad_heads = jnp.einsum("td,fd->tf", grad_attn, out_weight, preferred_element_type=jnp.float32)
    grad_heads = grad_heads.astype(jnp.bfloat16).reshape(images, LEN, heads_here, HD)
    scores_again = (
        jnp.einsum("gqhe,gkhe->ghqk", shaped[0], shaped[1], preferred_element_type=jnp.float32)
        / score_root
    )
    probs_again = jnp.exp(scores_again - log_total)
    grad_probs = jnp.einsum(
        "gqhe,gkhe->ghqk", grad_heads, shaped[2], preferred_element_type=jnp.float32
    )
    grad_scores = (
        probs_again * (grad_probs - jnp.sum(probs_again * grad_probs, axis=-1, keepdims=True))
    ).astype(jnp.bfloat16)
    grad_values = jnp.einsum(
        "ghqk,gqhe->gkhe",
        probs_again.astype(jnp.bfloat16),
        grad_heads,
        preferred_element_type=jnp.float32,
    )
    grad_queries = (
        jnp.einsum("ghqk,gkhe->gqhe", grad_scores, shaped[1], preferred_element_type=jnp.float32)
        / score_root
    )
    grad_keys = (
        jnp.einsum("ghqk,gqhe->gkhe", grad_scores, shaped[0], preferred_element_type=jnp.float32)
        / score_root
    )
    grad_qkv_rows = (
        jnp.stack([grad_queries, grad_keys, grad_values])
        .reshape(3, row_count, local_width)
        .astype(jnp.bfloat16)
    )
    grad_qkv = jnp.einsum(
        "td,stf->sdf", normed_one, grad_qkv_rows, preferred_element_type=jnp.float32
    )
    grad_normed_one = lax.psum(
        jnp.einsum("stf,sdf->td", grad_qkv_rows, qkv_weight, preferred_element_type=jnp.float32),
        "tensor",
    )
    input_back, grad_gain_attn = norm_back(grad_normed_one, unit_one, scale_one, gain_attn)
    grad_tokens = grad_residual + input_back
    squares = jnp.stack([jnp.sum(inputs * inputs), jnp.sum(attn * attn), jnp.sum(moe * moe)])
    summed = lax.psum(
        (grad_qkv, grad_out_weight, grad_gain_attn, grad_gain_moe, grad_router, squares), "expert"
    )
    entry_count = float(row_count * features * lax.axis_size("expert"))
    stats = jnp.sqrt(summed[5] / entry_count)
    return (
        result,
        grad_tokens,
        summed[0],
        summed[1],
        summed[2],
        summed[3],
        summed[4],
        grad_expert_in[None],
        grad_expert_out[None],
        stats,
    )


MOST_DENSE = 8


def dense_experts_kernel(
    x_ref, dy_ref, gate_ref, win_ref, wout_ref,
    moe_ref, dx_ref, gg_ref, gwin_ref, gwout_ref,
    moe_acc, dx_acc, gact_ref, gpre_ref,
):
    step = pl.program_id(0)
    chosen = step // 2

    @pl.when(step == 0)
    def _():
        moe_acc[...] = jnp.zeros_like(moe_acc)
        dx_acc[...] = jnp.zeros_like(dx_acc)
        gg_ref[...] = jnp.zeros_like(gg_ref)

    rows = x_ref.shape[0]
    chunk = rows // 4
    win = win_ref[0]
    wout = wout_ref[0]
    for c in range(4):
        part = pl.ds(c * chunk, chunk)
        pre = jnp.dot(x_ref[part, :], win, preferred_element_type=jnp.float32)
        back = lax.dot_general(
            dy_ref[part, :], wout, (((1,), (1,)), ((), ())), preferred_element_type=jnp.float32
        )
        half = 0.5 + 0.5 * lax.erf(pre * math.sqrt(0.5))
        act = pre * half
        slope = half + pre * (jnp.exp(pre * pre * -0.5) * (1.0 / math.sqrt(2.0 * math.pi)))
        lane = lax.broadcasted_iota(jnp.int32, (chunk, gate_ref.shape[1]), 1)
        mine = lane == chosen
        gate = jnp.sum(jnp.where(mine, gate_ref[part, :], 0.0), axis=1, keepdims=True)
        act = act.astype(jnp.bfloat16).astype(jnp.float32)
        seen = jnp.sum(act * back, axis=1, keepdims=True)
        gg_ref[part, :] = gg_ref[part, :] + jnp.where(mine, seen, 0.0)
        gact_ref[part, :] = (gate * act).astype(jnp.bfloat16)
        gpre_ref[part, :] = (gate * back * slope).astype(jnp.bfloat16)
    gact = gact_ref[...]
    gpre = gpre_ref[...]
    moe_acc[...] += jnp.dot(gact, wout, preferred_element_type=jnp.float32)
    dx_acc[...] += lax.dot_general(
        gpre, win, (((1,), (1,)), ((), ())), preferred_element_type=jnp.float32
    )
    gwin_ref[0] = lax.dot_general(
        x_ref[...], gpre, (((0,), (0,)), ((), ())), preferred_element_type=jnp.float32
    ).astype(gwin_ref.dtype)
    gwout_ref[0] = lax.dot_general(
        gact, dy_ref[...], (((0,), (0,)), ((), ())), preferred_element_type=jnp.float32
    ).astype(gwout_ref.dtype)

    @pl.when(step == pl.num_programs(0) - 1)
    def _():
        moe_ref[...] = moe_acc[...].astype(moe_ref.dtype)
        dx_ref[...] = dx_acc[...].astype(dx_ref.dtype)


def dense_experts(x, dy, gate, win, wout):
    rows, features = x.shape
    halves, _, hidden = win.shape
    experts = gate.shape[1]
    whole = lambda shape: pl.BlockSpec(shape, lambda j: (0,) * len(shape))
    return pl.pallas_call(
        dense_experts_kernel,
        grid=(halves,),
        in_specs=[
            whole((rows, features)),
            whole((rows, features)),
            whole((rows, experts)),
            pl.BlockSpec((1, features, hidden), lambda j: (j, 0, 0)),
            pl.BlockSpec((1, hidden, features), lambda j: (j, 0, 0)),
        ],
        out_specs=[
            whole((rows, features)),
            whole((rows, features)),
            whole((rows, experts)),
            pl.BlockSpec((1, features, hidden), lambda j: (j, 0, 0)),
            pl.BlockSpec((1, hidden, features), lambda j: (j, 0, 0)),
        ],
        out_shape=[
            jax.ShapeDtypeStruct((rows, features), jnp.bfloat16),
            jax.ShapeDtypeStruct((rows, features), jnp.bfloat16),
            jax.ShapeDtypeStruct((rows, experts), jnp.float32),
            jax.ShapeDtypeStruct((halves, features, hidden), jnp.bfloat16),
            jax.ShapeDtypeStruct((halves, hidden, features), jnp.bfloat16),
        ],
        scratch_shapes=[
            pltpu.VMEM((rows, features), jnp.float32),
            pltpu.VMEM((rows, features), jnp.float32),
            pltpu.VMEM((rows, hidden), jnp.bfloat16),
            pltpu.VMEM((rows, hidden), jnp.bfloat16),
        ],
        name="dense_experts",
    )(x, dy, gate, win, wout)


def kept_pairs(expert_ids, ranking, experts, capacity):
    iota = jnp.arange(experts, dtype=jnp.int32)[None, :]
    leading = (expert_ids[:, 0:1] == iota).astype(jnp.bfloat16)
    trailing = (expert_ids[:, 1:2] == iota).astype(jnp.bfloat16)
    earlier = (ranking[None, :] < ranking[:, None]).astype(jnp.bfloat16)
    before = jnp.dot(
        earlier, jnp.concatenate([leading, trailing], axis=1), preferred_element_type=jnp.float32
    )
    lead_f = leading.astype(jnp.float32)
    trail_f = trailing.astype(jnp.float32)
    lead_place = jnp.sum(before[:, :experts] * lead_f, axis=1)
    trail_place = jnp.sum((before[:, experts:] + jnp.sum(lead_f, axis=0)) * trail_f, axis=1)
    kept = jnp.stack([lead_place, trail_place], axis=1) < capacity
    return kept.astype(jnp.float32), lead_f, trail_f


def per_device_dense(
    tokens,
    qkv_weight,
    out_weight,
    gain_attn,
    gain_moe,
    router_weight,
    expert_in,
    expert_out,
    expert_ids,
    priority,
    cotangent,
):
    row_count, features = tokens.shape
    local_width = qkv_weight.shape[2]
    heads_here = local_width // HD
    images = row_count // LEN
    experts = router_weight.shape[1]
    capacity = max(2, 5 * row_count // (2 * experts))
    padded = -(-row_count // 32) * 32
    win_all = lax.all_gather(expert_in[0], "expert")
    wout_all = lax.all_gather(expert_out[0], "expert")
    kept, leading, trailing = kept_pairs(expert_ids, priority[0], experts, capacity)
    score_root = math.sqrt(HD)
    inputs = tokens.astype(jnp.float32)
    normed_one, unit_one, scale_one = norm_parts(inputs, gain_attn)
    normed_one = normed_one.astype(jnp.bfloat16)
    qkv = jnp.einsum(
        "td,sdf->stf", normed_one, qkv_weight, preferred_element_type=jnp.float32
    ).astype(jnp.bfloat16)
    shaped = qkv.reshape(3, images, LEN, heads_here, HD)
    scores = (
        jnp.einsum("gqhe,gkhe->ghqk", shaped[0], shaped[1], preferred_element_type=jnp.float32)
        / score_root
    )
    row_peak = jnp.max(scores, axis=-1, keepdims=True)
    weights = jnp.exp(scores - row_peak)
    weight_total = jnp.sum(weights, axis=-1, keepdims=True)
    probs = weights / weight_total
    log_total = row_peak + jnp.log(weight_total)
    head_rows = (
        jnp.einsum(
            "ghqk,gkhe->gqhe",
            probs.astype(jnp.bfloat16),
            shaped[2],
            preferred_element_type=jnp.float32,
        )
        .reshape(row_count, local_width)
        .astype(jnp.bfloat16)
    )
    attn = lax.psum(
        jnp.dot(head_rows, out_weight, preferred_element_type=jnp.float32).astype(jnp.bfloat16),
        "tensor",
    ).astype(jnp.float32)
    residual = inputs + attn
    normed_two, unit_two, scale_two = norm_parts(residual, gain_moe)
    normed_two = normed_two.astype(jnp.bfloat16)
    logits = jnp.dot(normed_two, router_weight, preferred_element_type=jnp.float32)
    chosen = jnp.stack(
        [jnp.sum(leading * logits, axis=1), jnp.sum(trailing * logits, axis=1)], axis=1
    )
    gates = jax.nn.softmax(chosen, axis=1)
    kept_gates = gates * kept
    spread_gates = leading * kept_gates[:, 0:1] + trailing * kept_gates[:, 1:2]
    pad = lambda v: jnp.pad(v, ((0, padded - row_count), (0, 0)))
    moe_part, back_part, gate_part, grad_in, grad_out = dense_experts(
        pad(normed_two), pad(cotangent), pad(spread_gates), win_all, wout_all
    )
    back_sum, gate_sum = lax.psum((back_part, gate_part), "tensor")
    moe = lax.psum(moe_part, "tensor")[:row_count].astype(jnp.float32)
    grad_expert_in = lax.psum_scatter(grad_in, "expert", scatter_dimension=0, tiled=True)
    grad_expert_out = lax.psum_scatter(grad_out, "expert", scatter_dimension=0, tiled=True)
    grad_y = cotangent.astype(jnp.float32)
    gate_sum = gate_sum[:row_count]
    gate_grad = kept * jnp.stack(
        [jnp.sum(leading * gate_sum, axis=1), jnp.sum(trailing * gate_sum, axis=1)], axis=1
    )
    result = (residual + moe).astype(jnp.bfloat16)
    grad_choice = gates * (gate_grad - jnp.sum(gates * gate_grad, axis=1, keepdims=True))
    grad_logits = leading * grad_choice[:, 0:1] + trailing * grad_choice[:, 1:2]
    grad_router = jnp.einsum(
        "td,te->de", normed_two.astype(jnp.float32), grad_logits, precision=HIGHEST
    )
    router_back = jnp.einsum(
        "te,de->td", grad_logits, router_weight.astype(jnp.float32), precision=HIGHEST
    )
    grad_normed_two = back_sum[:row_count].astype(jnp.float32) + router_back
    residual_back, grad_gain_moe = norm_back(grad_normed_two, unit_two, scale_two, gain_moe)
    grad_residual = grad_y + residual_back
    grad_attn = grad_residual.astype(jnp.bfloat16)
    grad_out_weight = jnp.einsum(
        "tf,td->fd", head_rows, grad_attn, preferred_element_type=jnp.float32
    )
    grad_heads = jnp.einsum("td,fd->tf", grad_attn, out_weight, preferred_element_type=jnp.float32)
    grad_heads = grad_heads.astype(jnp.bfloat16).reshape(images, LEN, heads_here, HD)
    scores_again = (
        jnp.einsum("gqhe,gkhe->ghqk", shaped[0], shaped[1], preferred_element_type=jnp.float32)
        / score_root
    )
    probs_again = jnp.exp(scores_again - log_total)
    grad_probs = jnp.einsum(
        "gqhe,gkhe->ghqk", grad_heads, shaped[2], preferred_element_type=jnp.float32
    )
    grad_scores = (
        probs_again * (grad_probs - jnp.sum(probs_again * grad_probs, axis=-1, keepdims=True))
    ).astype(jnp.bfloat16)
    grad_values = jnp.einsum(
        "ghqk,gqhe->gkhe",
        probs_again.astype(jnp.bfloat16),
        grad_heads,
        preferred_element_type=jnp.float32,
    )
    grad_queries = (
        jnp.einsum("ghqk,gkhe->gqhe", grad_scores, shaped[1], preferred_element_type=jnp.float32)
        / score_root
    )
    grad_keys = (
        jnp.einsum("ghqk,gqhe->gkhe", grad_scores, shaped[0], preferred_element_type=jnp.float32)
        / score_root
    )
    grad_qkv_rows = (
        jnp.stack([grad_queries, grad_keys, grad_values])
        .reshape(3, row_count, local_width)
        .astype(jnp.bfloat16)
    )
    grad_qkv = jnp.einsum(
        "td,stf->sdf", normed_one, grad_qkv_rows, preferred_element_type=jnp.float32
    )
    grad_normed_one = lax.psum(
        jnp.einsum(
            "stf,sdf->td", grad_qkv_rows, qkv_weight, preferred_element_type=jnp.float32
        ).astype(jnp.bfloat16),
        "tensor",
    ).astype(jnp.float32)
    input_back, grad_gain_attn = norm_back(grad_normed_one, unit_one, scale_one, gain_attn)
    grad_tokens = grad_residual + input_back
    squares = jnp.stack([jnp.sum(inputs * inputs), jnp.sum(attn * attn), jnp.sum(moe * moe)])
    summed = lax.psum(
        (grad_qkv, grad_out_weight, grad_gain_attn, grad_gain_moe, grad_router, squares), "expert"
    )
    entry_count = float(row_count * features * lax.axis_size("expert"))
    stats = jnp.sqrt(summed[5] / entry_count)
    return (
        result,
        grad_tokens,
        summed[0],
        summed[1],
        summed[2],
        summed[3],
        summed[4],
        grad_expert_in.astype(jnp.float32),
        grad_expert_out.astype(jnp.float32),
        stats,
    )


def solution(mesh):
    in_specs = (
        P("expert", None),
        P(None, None, "tensor"),
        P("tensor", None),
        P(),
        P(),
        P(),
        P("expert", None, "tensor"),
        P("expert", "tensor", None),
        P("expert", None),
        P("expert", None),
        P("expert", None),
    )
    out_specs = (
        P("expert", None),
        P("expert", None),
        P(None, None, "tensor"),
        P("tensor", None),
        P(),
        P(),
        P(),
        P("expert", None, "tensor"),
        P("expert", "tensor", None),
        P(),
    )
    few = 2 * MOST_DENSE >= mesh.shape["expert"]
    return jax.shard_map(
        per_device_dense if few else per_device_slots, mesh=mesh, in_specs=in_specs, out_specs=out_specs, check_vma=False
    )
```

```python
import math

import jax
import jax.numpy as jnp
from jax import lax
from jax.experimental import pallas as pl
from jax.experimental.pallas import tpu as pltpu
from jax.sharding import PartitionSpec as P

HD = 64
LEN = 197


EPSILON = 1e-06
HIGHEST = lax.Precision.HIGHEST


def slot_table(expert_ids, ranking, experts, capacity):
    count = expert_ids.shape[0]
    ordering = jnp.zeros((count,), jnp.int32).at[ranking].set(jnp.arange(count, dtype=jnp.int32))
    expert_iota = jnp.arange(experts, dtype=jnp.int32)
    leading = (expert_ids[:, 0:1] == expert_iota[None, :]).astype(jnp.int32)
    trailing = (expert_ids[:, 1:2] == expert_iota[None, :]).astype(jnp.int32)
    lead_sorted = leading[ordering]
    trail_sorted = trailing[ordering]
    lead_before = (jnp.cumsum(lead_sorted, axis=0) - lead_sorted)[ranking]
    trail_before = (jnp.cumsum(trail_sorted, axis=0) - trail_sorted)[ranking] + jnp.sum(
        leading, axis=0
    )[None, :]
    lead_place = jnp.sum(lead_before * leading, axis=1)
    trail_place = jnp.sum(trail_before * trailing, axis=1)
    placing = jnp.stack([lead_place, trail_place], axis=1)
    return jnp.where(placing < capacity, expert_ids * capacity + placing, experts * capacity)


def norm_parts(values, gain):
    scaling = lax.rsqrt(jnp.mean(values * values, axis=-1, keepdims=True) + EPSILON)
    unit_rows = values * scaling
    return (unit_rows * gain, unit_rows, scaling)


def norm_back(incoming, unit_rows, scaling, gain):
    inner = incoming * gain
    spread_back = scaling * (
        inner - unit_rows * jnp.mean(inner * unit_rows, axis=-1, keepdims=True)
    )
    return (spread_back, jnp.sum(incoming * unit_rows, axis=0))


def pair_tables(slot_block, slot_count):
    slot_iota = jnp.arange(slot_count, dtype=jnp.int32)[None, :]
    return (
        (slot_block[:, 0:1] == slot_iota).astype(jnp.bfloat16),
        (slot_block[:, 1:2] == slot_iota).astype(jnp.bfloat16),
    )


def to_experts(buffer):
    doubled = jnp.repeat(buffer, 2, axis=0)
    moved = lax.all_to_all(doubled, "expert", split_axis=0, concat_axis=0, tiled=True)
    return moved.reshape(moved.shape[0] * moved.shape[1], moved.shape[2])


def tensor_total(summand):
    return lax.psum(summand, "tensor")


def from_experts(rows_back, experts, capacity):
    shaped_back = rows_back.reshape(2 * experts, capacity, rows_back.shape[1])
    moved = lax.all_to_all(shaped_back, "expert", split_axis=0, concat_axis=0, tiled=True)
    width = moved.shape[2]
    halves = jnp.sum(moved.reshape(experts, 2, capacity, width), axis=1)
    return halves.astype(jnp.bfloat16).reshape(experts * capacity, width)


def per_device_slots(
    tokens,
    qkv_weight,
    out_weight,
    gain_attn,
    gain_moe,
    router_weight,
    expert_in,
    expert_out,
    expert_ids,
    priority,
    cotangent,
):
    row_count, features = tokens.shape
    local_width = qkv_weight.shape[2]
    heads_here = local_width // HD
    images = row_count // LEN
    experts = router_weight.shape[1]
    capacity = max(2, 5 * row_count // (2 * experts))
    slot_count = experts * capacity
    block_rows = 2 * LEN
    blocks = row_count // block_rows
    slot_index = slot_table(expert_ids, priority[0], experts, capacity)
    slot_blocks = slot_index.reshape(blocks, block_rows, 2)
    score_root = math.sqrt(HD)
    inputs = tokens.astype(jnp.float32)
    normed_one, unit_one, scale_one = norm_parts(inputs, gain_attn)
    normed_one = normed_one.astype(jnp.bfloat16)
    qkv = jnp.einsum(
        "td,sdf->stf", normed_one, qkv_weight, preferred_element_type=jnp.float32
    ).astype(jnp.bfloat16)
    shaped = qkv.reshape(3, images, LEN, heads_here, HD)
    scores = (
        jnp.einsum("gqhe,gkhe->ghqk", shaped[0], shaped[1], preferred_element_type=jnp.float32)
        / score_root
    )
    row_peak = jnp.max(scores, axis=-1, keepdims=True)
    weights = jnp.exp(scores - row_peak)
    weight_total = jnp.sum(weights, axis=-1, keepdims=True)
    probs = weights / weight_total
    log_total = row_peak + jnp.log(weight_total)
    head_rows = (
        jnp.einsum(
            "ghqk,gkhe->gqhe",
            probs.astype(jnp.bfloat16),
            shaped[2],
            preferred_element_type=jnp.float32,
        )
        .reshape(row_count, local_width)
        .astype(jnp.bfloat16)
    )
    attn = lax.psum(jnp.dot(head_rows, out_weight, preferred_element_type=jnp.float32), "tensor")
    residual = inputs + attn
    normed_two, unit_two, scale_two = norm_parts(residual, gain_moe)
    normed_two = normed_two.astype(jnp.bfloat16)
    logits = jnp.dot(normed_two, router_weight, preferred_element_type=jnp.float32)
    expert_iota = jnp.arange(experts, dtype=jnp.int32)
    choosing = (expert_ids[:, :, None] == expert_iota[None, None, :]).astype(jnp.float32)
    chosen = jnp.sum(choosing * logits[:, None, :], axis=2)
    gates = jax.nn.softmax(chosen, axis=1)

    def collect(carry, element):
        leading, trailing = pair_tables(element[0], slot_count)
        return (
            carry
            + jnp.einsum(
                "tc,td->cd", leading + trailing, element[1], preferred_element_type=jnp.float32
            ),
            None,
        )

    dispatched, ignored = lax.scan(
        collect,
        jnp.zeros((slot_count, features), jnp.float32),
        (slot_blocks, normed_two.reshape(blocks, block_rows, features)),
    )
    dispatched = dispatched.astype(jnp.bfloat16).reshape(experts, capacity, features)
    received = to_experts(dispatched)
    pre_act = jnp.dot(received, expert_in[0], preferred_element_type=jnp.float32)
    activated = jax.nn.gelu(pre_act, approximate=False).astype(jnp.bfloat16)
    returned = from_experts(
        tensor_total(jnp.dot(activated, expert_out[0], preferred_element_type=jnp.float32)),
        experts,
        capacity,
    )
    grad_y = cotangent.astype(jnp.float32)

    def combine(carry, element):
        slot_block, gate_block, grad_block = element
        leading, trailing = pair_tables(slot_block, slot_count)
        got_lead = jnp.dot(leading, returned, preferred_element_type=jnp.float32)
        got_trail = jnp.dot(trailing, returned, preferred_element_type=jnp.float32)
        mixed = gate_block[:, 0:1] * got_lead + gate_block[:, 1:2] * got_trail
        gate_grad = jnp.stack(
            [jnp.sum(grad_block * got_lead, axis=1), jnp.sum(grad_block * got_trail, axis=1)],
            axis=1,
        )
        carry = carry + jnp.einsum(
            "tc,td->cd",
            leading,
            (gate_block[:, 0:1] * grad_block).astype(jnp.bfloat16),
            preferred_element_type=jnp.float32,
        )
        carry = carry + jnp.einsum(
            "tc,td->cd",
            trailing,
            (gate_block[:, 1:2] * grad_block).astype(jnp.bfloat16),
            preferred_element_type=jnp.float32,
        )
        return (carry, (mixed, gate_grad))

    grad_slots, (moe, gate_grad) = lax.scan(
        combine,
        jnp.zeros((slot_count, features), jnp.float32),
        (
            slot_blocks,
            gates.reshape(blocks, block_rows, 2),
            grad_y.reshape(blocks, block_rows, features),
        ),
    )
    moe = moe.reshape(row_count, features)
    gate_grad = gate_grad.reshape(row_count, 2)
    result = (residual + moe).astype(jnp.bfloat16)
    grad_rows = to_experts(grad_slots.astype(jnp.bfloat16).reshape(experts, capacity, features))
    grad_act = jnp.einsum("rd,fd->rf", grad_rows, expert_out[0], preferred_element_type=jnp.float32)
    ignored, gelu_back = jax.vjp(lambda values: jax.nn.gelu(values, approximate=False), pre_act)
    grad_pre = gelu_back(grad_act)[0].astype(jnp.bfloat16)
    grad_expert_out = jnp.einsum(
        "rf,rd->fd", activated, grad_rows, preferred_element_type=jnp.float32
    )
    grad_expert_in = jnp.einsum("rd,rf->df", received, grad_pre, preferred_element_type=jnp.float32)
    grad_sent = from_experts(
        tensor_total(
            jnp.einsum("rf,df->rd", grad_pre, expert_in[0], preferred_element_type=jnp.float32)
        ),
        experts,
        capacity,
    )
    grad_choice = gates * (gate_grad - jnp.sum(gates * gate_grad, axis=1, keepdims=True))
    grad_logits = jnp.sum(choosing * grad_choice[:, :, None], axis=1)
    grad_router = jnp.einsum(
        "td,te->de", normed_two.astype(jnp.float32), grad_logits, precision=HIGHEST
    )
    router_back = jnp.einsum(
        "te,de->td", grad_logits, router_weight.astype(jnp.float32), precision=HIGHEST
    )

    def spread_rows(slot_block):
        leading, trailing = pair_tables(slot_block, slot_count)
        return jnp.dot(leading + trailing, grad_sent, preferred_element_type=jnp.float32)

    grad_normed_two = lax.map(spread_rows, slot_blocks).reshape(row_count, features) + router_back
    residual_back, grad_gain_moe = norm_back(grad_normed_two, unit_two, scale_two, gain_moe)
    grad_residual = grad_y + residual_back
    grad_attn = grad_residual.astype(jnp.bfloat16)
    grad_out_weight = jnp.einsum(
        "tf,td->fd", head_rows, grad_attn, preferred_element_type=jnp.float32
    )
    grad_heads = jnp.einsum("td,fd->tf", grad_attn, out_weight, preferred_element_type=jnp.float32)
    grad_heads = grad_heads.astype(jnp.bfloat16).reshape(images, LEN, heads_here, HD)
    scores_again = (
        jnp.einsum("gqhe,gkhe->ghqk", shaped[0], shaped[1], preferred_element_type=jnp.float32)
        / score_root
    )
    probs_again = jnp.exp(scores_again - log_total)
    grad_probs = jnp.einsum(
        "gqhe,gkhe->ghqk", grad_heads, shaped[2], preferred_element_type=jnp.float32
    )
    grad_scores = (
        probs_again * (grad_probs - jnp.sum(probs_again * grad_probs, axis=-1, keepdims=True))
    ).astype(jnp.bfloat16)
    grad_values = jnp.einsum(
        "ghqk,gqhe->gkhe",
        probs_again.astype(jnp.bfloat16),
        grad_heads,
        preferred_element_type=jnp.float32,
    )
    grad_queries = (
        jnp.einsum("ghqk,gkhe->gqhe", grad_scores, shaped[1], preferred_element_type=jnp.float32)
        / score_root
    )
    grad_keys = (
        jnp.einsum("ghqk,gqhe->gkhe", grad_scores, shaped[0], preferred_element_type=jnp.float32)
        / score_root
    )
    grad_qkv_rows = (
        jnp.stack([grad_queries, grad_keys, grad_values])
        .reshape(3, row_count, local_width)
        .astype(jnp.bfloat16)
    )
    grad_qkv = jnp.einsum(
        "td,stf->sdf", normed_one, grad_qkv_rows, preferred_element_type=jnp.float32
    )
    grad_normed_one = lax.psum(
        jnp.einsum("stf,sdf->td", grad_qkv_rows, qkv_weight, preferred_element_type=jnp.float32),
        "tensor",
    )
    input_back, grad_gain_attn = norm_back(grad_normed_one, unit_one, scale_one, gain_attn)
    grad_tokens = grad_residual + input_back
    squares = jnp.stack([jnp.sum(inputs * inputs), jnp.sum(attn * attn), jnp.sum(moe * moe)])
    summed = lax.psum(
        (grad_qkv, grad_out_weight, grad_gain_attn, grad_gain_moe, grad_router, squares), "expert"
    )
    entry_count = float(row_count * features * lax.axis_size("expert"))
    stats = jnp.sqrt(summed[5] / entry_count)
    return (
        result,
        grad_tokens,
        summed[0],
        summed[1],
        summed[2],
        summed[3],
        summed[4],
        grad_expert_in[None],
        grad_expert_out[None],
        stats,
    )


def stage_pairs(moves):
    return [(2 * a + x, 2 * b + x) for a, b in moves for x in range(2)]


TO_RIGHT = stage_pairs([(0, 1), (1, 2), (2, 3)])
TO_LEFT = stage_pairs([(1, 0), (2, 1), (3, 2)])
ACROSS = [(i, i ^ 1) for i in range(8)]


def mixed(a, b):
    return (a.astype(jnp.float32) + b.astype(jnp.float32)).astype(jnp.bfloat16)


def spread_weights(own, place):
    send = lambda v, pairs: lax.ppermute(v, "expert", pairs)
    right = send(own, TO_RIGHT)
    left = send(own, TO_LEFT)
    cross_own = send(own, ACROSS)
    near = jnp.where(place >= 1, right, left)
    cross_near = send(near, ACROSS)
    right_two = send(right, stage_pairs([(1, 2), (2, 3)]))
    left_two = send(left, stage_pairs([(1, 0), (2, 1)]))
    middle = jnp.where(place >= 2, right_two, left_two)
    cross_middle = send(middle, ACROSS)
    end = send(middle, stage_pairs([(2, 3), (1, 0)]))
    far = jnp.where((place == 1) | (place == 2), left, end)
    cross_far = send(far, ACROSS)
    return [own, near, middle, far, cross_own, cross_near, cross_middle, cross_far]


def gather_grads(blocks, place):
    send = lambda v, pairs: lax.ppermute(v, "expert", pairs)
    own, near, middle, far, their_own, their_near, their_middle, their_far = blocks
    far = mixed(far, send(their_far, ACROSS))
    middle = mixed(middle, send(their_middle, ACROSS))
    near = mixed(near, send(their_near, ACROSS))
    their_own = send(their_own, ACROSS)
    end = send(far, stage_pairs([(0, 1), (3, 2)]))
    middle = mixed(middle, end)
    right_two = send(middle, stage_pairs([(0, 1), (1, 2)]))
    left_two = send(middle, stage_pairs([(3, 2), (2, 1)]))
    right = send(jnp.where(place == 0, near, mixed(far, right_two)), TO_RIGHT)
    left = send(mixed(near, left_two), TO_LEFT)
    wide = lambda v: v.astype(jnp.float32)
    return (wide(own) + wide(their_own)) + (wide(right) + wide(left))


def flipped(parts, bits, index):
    shape = parts.shape
    parts = parts.reshape((2,) * bits + shape[1:])
    for b in range(bits):
        is_set = ((index >> (bits - 1 - b)) & 1) == 1
        parts = jnp.where(is_set, jnp.flip(parts, axis=b), parts)
    return parts.reshape(shape)


def flip_pairs(count, mask):
    return [(i, i ^ mask) for i in range(count)]


def quarter_sum(parts, t):
    part = lambda k: lax.dynamic_index_in_dim(parts, t ^ k, 0, keepdims=False)
    got = lax.ppermute(jnp.stack([part(1), part(3)]), "tensor", flip_pairs(4, 1))
    wide = lambda v: v.astype(jnp.float32)
    other = lax.ppermute(mixed(part(2), got[1]), "tensor", flip_pairs(4, 2))
    return (wide(part(0)) + wide(got[0])) + wide(other)


def quarter_spread(own, t):
    other = lax.ppermute(own, "tensor", flip_pairs(4, 2))
    pair = jnp.stack([own, other])
    got = lax.ppermute(pair, "tensor", flip_pairs(4, 1))
    return flipped(jnp.stack([pair[0], got[0], pair[1], got[1]]), 2, t)


def total_small(v):
    for mask in (1, 2):
        v = v + lax.ppermute(v, "tensor", flip_pairs(4, mask))
    parts = [lax.ppermute(v, "expert", flip_pairs(8, mask)) for mask in range(1, 8)]
    return v + sum(parts)


def total_blocks(blocks, d):
    part = lambda k: lax.dynamic_index_in_dim(blocks, d ^ k, 0, keepdims=False)
    got = [lax.ppermute(part(k), "expert", flip_pairs(8, k)) for k in range(1, 8)]
    mine = part(0).astype(jnp.float32)
    for v in got:
        mine = mine + v.astype(jnp.float32)
    mine = mine.astype(jnp.bfloat16)
    back = [lax.ppermute(mine, "expert", flip_pairs(8, k)) for k in range(1, 8)]
    return flipped(jnp.stack([mine] + back), 3, d).astype(jnp.float32)


def dense_experts_kernel(
    which_ref, x_ref, dy_ref, gate_ref, *refs,
):
    w_refs = refs[:8]
    moe_ref, dx_ref = refs[8:10]
    g_refs = refs[10:18]
    w_now, moe_acc, dx_acc, gg_acc, gact_ref, gpre_ref, g_now = refs[18:]
    step = pl.program_id(0)
    chosen = which_ref[step]

    @pl.when(step == 0)
    def _():
        moe_acc[...] = jnp.zeros_like(moe_acc)
        dx_acc[...] = jnp.zeros_like(dx_acc)
        gg_acc[...] = jnp.zeros_like(gg_acc)

    for k in range(8):

        @pl.when(step == k)
        def _():
            w_now[...] = w_refs[k][...]

    rows = x_ref.shape[0]
    chunk = rows // 4
    win = w_now[0]
    wout = w_now[1]
    for c in range(4):
        part = pl.ds(c * chunk, chunk)
        pre = jnp.dot(x_ref[part, :], win, preferred_element_type=jnp.float32)
        back = jnp.dot(dy_ref[part, :], wout, preferred_element_type=jnp.float32)
        half = 0.5 + 0.5 * lax.erf(pre * math.sqrt(0.5))
        act = pre * half
        slope = half + pre * (jnp.exp(pre * pre * -0.5) * (1.0 / math.sqrt(2.0 * math.pi)))
        lane = lax.broadcasted_iota(jnp.int32, (chunk, 128), 1)
        mine = lane == chosen
        lane_in = lax.broadcasted_iota(jnp.int32, (chunk, gate_ref.shape[1]), 1)
        gate = jnp.sum(
            jnp.where(lane_in == chosen, gate_ref[part, :], 0.0), axis=1, keepdims=True
        )
        act = act.astype(jnp.bfloat16).astype(jnp.float32)
        seen = jnp.sum(act * back, axis=1, keepdims=True)
        gg_acc[part, :] = gg_acc[part, :] + jnp.where(mine, seen, 0.0)
        gact_ref[part, :] = (gate * act).astype(jnp.bfloat16)
        gpre_ref[part, :] = (gate * back * slope).astype(jnp.bfloat16)
    gact = gact_ref[...]
    gpre = gpre_ref[...]
    moe_acc[...] += lax.dot_general(
        gact, wout, (((1,), (1,)), ((), ())), preferred_element_type=jnp.float32
    )
    dx_acc[...] += lax.dot_general(
        gpre, win, (((1,), (1,)), ((), ())), preferred_element_type=jnp.float32
    )
    g_now[0] = lax.dot_general(
        x_ref[...], gpre, (((0,), (0,)), ((), ())), preferred_element_type=jnp.float32
    ).astype(jnp.bfloat16)
    g_now[1] = lax.dot_general(
        dy_ref[...], gact, (((0,), (0,)), ((), ())), preferred_element_type=jnp.float32
    ).astype(jnp.bfloat16)
    for k in range(8):

        @pl.when(step == k)
        def _():
            g_refs[k][...] = g_now[...]

    @pl.when(step == 7)
    def _():
        features = x_ref.shape[1]
        moe_ref[...] = moe_acc[...].astype(jnp.bfloat16)
        dx_ref[:, :features] = dx_acc[...].astype(jnp.bfloat16)
        high = gg_acc[...].astype(jnp.bfloat16).astype(jnp.float32)
        rest = pltpu.roll(gg_acc[...] - high, 64, axis=1)
        dx_ref[:, features:] = (high + rest).astype(jnp.bfloat16)


def dense_experts(which, x, dy, gate, blocks):
    rows, features = x.shape
    hidden = blocks[0].shape[2]
    experts = gate.shape[1]
    whole = lambda shape: pl.BlockSpec(shape, lambda j, w: (0,) * len(shape))
    one = (2, features, hidden)
    outs = pl.pallas_call(
        dense_experts_kernel,
        grid_spec=pltpu.PrefetchScalarGridSpec(
            num_scalar_prefetch=1,
            grid=(8,),
            in_specs=[whole((rows, features)), whole((rows, features)), whole((rows, experts))]
            + [whole(one)] * 8,
            out_specs=[whole((rows, features)), whole((rows, features + 128))] + [whole(one)] * 8,
            scratch_shapes=[
                pltpu.VMEM(one, jnp.bfloat16),
                pltpu.VMEM((rows, features), jnp.float32),
                pltpu.VMEM((rows, features), jnp.float32),
                pltpu.VMEM((rows, 128), jnp.float32),
                pltpu.VMEM((rows, hidden), jnp.bfloat16),
                pltpu.VMEM((rows, hidden), jnp.bfloat16),
                pltpu.VMEM(one, jnp.bfloat16),
            ],
        ),
        out_shape=[
            jax.ShapeDtypeStruct((rows, features), jnp.bfloat16),
            jax.ShapeDtypeStruct((rows, features + 128), jnp.bfloat16),
        ]
        + [jax.ShapeDtypeStruct(one, jnp.bfloat16)] * 8,
        name="dense_experts",
    )(which, x, dy, gate, *blocks)
    return outs[0], outs[1], outs[2:]


def kept_pairs(expert_ids, ranking, experts, capacity):
    iota = jnp.arange(experts, dtype=jnp.int32)[None, :]
    leading = (expert_ids[:, 0:1] == iota).astype(jnp.bfloat16)
    trailing = (expert_ids[:, 1:2] == iota).astype(jnp.bfloat16)
    earlier = (ranking[None, :] < ranking[:, None]).astype(jnp.bfloat16)
    before = jnp.dot(
        earlier, jnp.concatenate([leading, trailing], axis=1), preferred_element_type=jnp.float32
    )
    lead_f = leading.astype(jnp.float32)
    trail_f = trailing.astype(jnp.float32)
    lead_place = jnp.sum(before[:, :experts] * lead_f, axis=1)
    trail_place = jnp.sum((before[:, experts:] + jnp.sum(lead_f, axis=0)) * trail_f, axis=1)
    kept = jnp.stack([lead_place, trail_place], axis=1) < capacity
    return kept.astype(jnp.float32), lead_f, trail_f


def per_device_dense(
    tokens,
    qkv_weight,
    out_weight,
    gain_attn,
    gain_moe,
    router_weight,
    expert_in,
    expert_out,
    expert_ids,
    priority,
    cotangent,
):
    row_count, features = tokens.shape
    local_width = qkv_weight.shape[2]
    heads_here = local_width // HD
    images = row_count // LEN
    experts = router_weight.shape[1]
    capacity = max(2, 5 * row_count // (2 * experts))
    padded = -(-row_count // 32) * 32
    quarter = padded // 4
    t = lax.axis_index("tensor")
    d = lax.axis_index("expert")
    place = d // 2
    slot_places = jnp.stack(
        [
            place,
            jnp.where(place >= 1, place - 1, 1),
            place ^ 2,
            jnp.where(place == 1, 2, jnp.where(place == 3, 0, 3)),
        ]
    )
    which = jnp.concatenate([slot_places, slot_places]).astype(jnp.int32)
    pad = lambda v: jnp.pad(v, ((0, padded - row_count), (0, 0)))
    mine = lambda v: lax.dynamic_slice_in_dim(pad(v), t * quarter, quarter, 0)
    blocks = spread_weights(jnp.stack([expert_in[0], expert_out[0].T]), place)
    kept, leading, trailing = kept_pairs(expert_ids, priority[0], experts, capacity)
    score_root = math.sqrt(HD)
    inputs = tokens.astype(jnp.float32)
    normed_one, unit_one, scale_one = norm_parts(inputs, gain_attn)
    normed_one = normed_one.astype(jnp.bfloat16)
    qkv = jnp.einsum(
        "td,sdf->stf", normed_one, qkv_weight, preferred_element_type=jnp.float32
    ).astype(jnp.bfloat16)
    shaped = qkv.reshape(3, images, LEN, heads_here, HD)
    scores = (
        jnp.einsum("gqhe,gkhe->ghqk", shaped[0], shaped[1], preferred_element_type=jnp.float32)
        / score_root
    )
    row_peak = jnp.max(scores, axis=-1, keepdims=True)
    weights = jnp.exp(scores - row_peak)
    weight_total = jnp.sum(weights, axis=-1, keepdims=True)
    probs = weights / weight_total
    log_total = row_peak + jnp.log(weight_total)
    head_rows = (
        jnp.einsum(
            "ghqk,gkhe->gqhe",
            probs.astype(jnp.bfloat16),
            shaped[2],
            preferred_element_type=jnp.float32,
        )
        .reshape(row_count, local_width)
        .astype(jnp.bfloat16)
    )
    attn_part = jnp.dot(pad(head_rows), out_weight, preferred_element_type=jnp.float32)
    attn = quarter_sum(attn_part.astype(jnp.bfloat16).reshape(4, quarter, features), t)
    inputs_here = mine(tokens).astype(jnp.float32)
    residual = inputs_here + attn
    normed_two, unit_two, scale_two = norm_parts(residual, gain_moe)
    normed_two = normed_two.astype(jnp.bfloat16)
    all_normed = quarter_spread(normed_two, t).reshape(padded, features)
    softmax_gates = lambda lead, trail, logits: jax.nn.softmax(
        jnp.stack([jnp.sum(lead * logits, axis=1), jnp.sum(trail * logits, axis=1)], axis=1),
        axis=1,
    )
    logits = jnp.dot(all_normed, router_weight, preferred_element_type=jnp.float32)
    all_gates = softmax_gates(pad(leading), pad(trailing), logits)
    kept_gates = all_gates * pad(kept)
    spread_gates = pad(leading) * kept_gates[:, 0:1] + pad(trailing) * kept_gates[:, 1:2]
    moe_part, back_part, grads = dense_experts(
        which, all_normed, pad(cotangent), spread_gates, blocks
    )
    back_sum = quarter_sum(back_part.reshape(4, quarter, features + 128), t)
    moe = quarter_sum(moe_part.reshape(4, quarter, features), t)
    grad_expert = gather_grads(grads, place)
    lead_here, trail_here, kept_here = mine(leading), mine(trailing), mine(kept)
    gates = lax.dynamic_slice_in_dim(all_gates, t * quarter, quarter, 0)
    grad_y = mine(cotangent).astype(jnp.float32)
    gate_sum = (
        back_sum[:, features : features + experts]
        + back_sum[:, features + 64 : features + 64 + experts]
    )
    gate_grad = kept_here * jnp.stack(
        [jnp.sum(lead_here * gate_sum, axis=1), jnp.sum(trail_here * gate_sum, axis=1)], axis=1
    )
    result = (residual + moe).astype(jnp.bfloat16)
    grad_choice = gates * (gate_grad - jnp.sum(gates * gate_grad, axis=1, keepdims=True))
    grad_logits = lead_here * grad_choice[:, 0:1] + trail_here * grad_choice[:, 1:2]
    grad_router = jnp.einsum(
        "td,te->ed", normed_two.astype(jnp.float32), grad_logits, precision=HIGHEST
    )
    router_back = jnp.einsum(
        "te,de->td", grad_logits, router_weight.astype(jnp.float32), precision=HIGHEST
    )
    grad_normed_two = back_sum[:, :features] + router_back
    residual_back, grad_gain_moe = norm_back(grad_normed_two, unit_two, scale_two, gain_moe)
    grad_residual = grad_y + residual_back
    grad_attn = quarter_spread(grad_residual.astype(jnp.bfloat16), t).reshape(padded, features)[
        :row_count
    ]
    grad_out_turned = jnp.einsum(
        "td,tf->df", grad_attn, head_rows, preferred_element_type=jnp.float32
    )
    grad_heads = jnp.einsum("td,fd->tf", grad_attn, out_weight, preferred_element_type=jnp.float32)
    grad_heads = grad_heads.astype(jnp.bfloat16).reshape(images, LEN, heads_here, HD)
    scores_again = (
        jnp.einsum("gqhe,gkhe->ghqk", shaped[0], shaped[1], preferred_element_type=jnp.float32)
        / score_root
    )
    probs_again = jnp.exp(scores_again - log_total)
    grad_probs = jnp.einsum(
        "gqhe,gkhe->ghqk", grad_heads, shaped[2], preferred_element_type=jnp.float32
    )
    grad_scores = (
        probs_again * (grad_probs - jnp.sum(probs_again * grad_probs, axis=-1, keepdims=True))
    ).astype(jnp.bfloat16)
    grad_values = jnp.einsum(
        "ghqk,gqhe->gkhe",
        probs_again.astype(jnp.bfloat16),
        grad_heads,
        preferred_element_type=jnp.float32,
    )
    grad_queries = (
        jnp.einsum("ghqk,gkhe->gqhe", grad_scores, shaped[1], preferred_element_type=jnp.float32)
        / score_root
    )
    grad_keys = (
        jnp.einsum("ghqk,gqhe->gkhe", grad_scores, shaped[0], preferred_element_type=jnp.float32)
        / score_root
    )
    grad_qkv_rows = (
        jnp.stack([grad_queries, grad_keys, grad_values])
        .reshape(3, row_count, local_width)
        .astype(jnp.bfloat16)
    )
    grad_qkv = jnp.einsum(
        "td,stf->sdf", normed_one, grad_qkv_rows, preferred_element_type=jnp.float32
    )
    normed_back = jnp.einsum(
        "stf,sdf->td", grad_qkv_rows, qkv_weight, preferred_element_type=jnp.float32
    ).astype(jnp.bfloat16)
    grad_normed_one = quarter_sum(pad(normed_back).reshape(4, quarter, features), t)
    _, unit_here, scale_here = norm_parts(inputs_here, gain_attn)
    input_back, grad_gain_attn = norm_back(grad_normed_one, unit_here, scale_here, gain_attn)
    grad_tokens = quarter_spread((grad_residual + input_back).astype(jnp.bfloat16), t)
    grad_tokens = grad_tokens.reshape(padded, features)[:row_count].astype(jnp.float32)
    result = quarter_spread(result, t).reshape(padded, features)[:row_count]
    squares = jnp.stack(
        [jnp.sum(inputs_here * inputs_here), jnp.sum(attn * attn), jnp.sum(moe * moe)]
    )
    small = jnp.concatenate(
        [
            grad_gain_attn[None],
            grad_gain_moe[None],
            grad_router,
            jnp.pad(squares, (0, features - 3))[None],
        ]
    )
    small = total_small(small)
    weight_grads = jnp.concatenate([grad_qkv, grad_out_turned[None]]).astype(jnp.bfloat16)
    weight_grads = total_blocks(weight_grads.reshape(8, features // 2, local_width), d)
    weight_grads = weight_grads.reshape(4, features, local_width)
    entry_count = float(row_count * features * lax.axis_size("expert"))
    stats = jnp.sqrt(small[2 + experts, :3] / entry_count)
    return (
        result,
        grad_tokens,
        weight_grads[:3],
        weight_grads[3].T,
        small[0],
        small[1],
        small[2 : 2 + experts].T,
        grad_expert[0][None],
        grad_expert[1].T[None],
        stats,
    )


def solution(mesh):
    in_specs = (
        P("expert", None),
        P(None, None, "tensor"),
        P("tensor", None),
        P(),
        P(),
        P(),
        P("expert", None, "tensor"),
        P("expert", "tensor", None),
        P("expert", None),
        P("expert", None),
        P("expert", None),
    )
    out_specs = (
        P("expert", None),
        P("expert", None),
        P(None, None, "tensor"),
        P("tensor", None),
        P(),
        P(),
        P(),
        P("expert", None, "tensor"),
        P("expert", "tensor", None),
        P(),
    )
    few = mesh.shape["expert"] == 8 and mesh.shape["tensor"] == 4
    return jax.shard_map(
        per_device_dense if few else per_device_slots, mesh=mesh, in_specs=in_specs, out_specs=out_specs, check_vma=False
    )
```

```python
import functools
import math

import jax
import jax.numpy as jnp
from jax import lax
from jax.experimental import pallas as pl
from jax.experimental.pallas import tpu as pltpu
from jax.sharding import PartitionSpec as P

HD = 64
LEN = 197


EPSILON = 1e-06
HIGHEST = lax.Precision.HIGHEST


def slot_table(expert_ids, ranking, experts, capacity):
    count = expert_ids.shape[0]
    ordering = jnp.zeros((count,), jnp.int32).at[ranking].set(jnp.arange(count, dtype=jnp.int32))
    expert_iota = jnp.arange(experts, dtype=jnp.int32)
    leading = (expert_ids[:, 0:1] == expert_iota[None, :]).astype(jnp.int32)
    trailing = (expert_ids[:, 1:2] == expert_iota[None, :]).astype(jnp.int32)
    lead_sorted = leading[ordering]
    trail_sorted = trailing[ordering]
    lead_before = (jnp.cumsum(lead_sorted, axis=0) - lead_sorted)[ranking]
    trail_before = (jnp.cumsum(trail_sorted, axis=0) - trail_sorted)[ranking] + jnp.sum(
        leading, axis=0
    )[None, :]
    lead_place = jnp.sum(lead_before * leading, axis=1)
    trail_place = jnp.sum(trail_before * trailing, axis=1)
    placing = jnp.stack([lead_place, trail_place], axis=1)
    return jnp.where(placing < capacity, expert_ids * capacity + placing, experts * capacity)


def norm_parts(values, gain):
    scaling = lax.rsqrt(jnp.mean(values * values, axis=-1, keepdims=True) + EPSILON)
    unit_rows = values * scaling
    return (unit_rows * gain, unit_rows, scaling)


def norm_back(incoming, unit_rows, scaling, gain):
    inner = incoming * gain
    spread_back = scaling * (
        inner - unit_rows * jnp.mean(inner * unit_rows, axis=-1, keepdims=True)
    )
    return (spread_back, jnp.sum(incoming * unit_rows, axis=0))


def pair_tables(slot_block, slot_count):
    slot_iota = jnp.arange(slot_count, dtype=jnp.int32)[None, :]
    return (
        (slot_block[:, 0:1] == slot_iota).astype(jnp.bfloat16),
        (slot_block[:, 1:2] == slot_iota).astype(jnp.bfloat16),
    )


def to_experts(buffer):
    doubled = jnp.repeat(buffer, 2, axis=0)
    moved = lax.all_to_all(doubled, "expert", split_axis=0, concat_axis=0, tiled=True)
    return moved.reshape(moved.shape[0] * moved.shape[1], moved.shape[2])


def tensor_total(summand):
    return lax.psum(summand, "tensor")


def from_experts(rows_back, experts, capacity):
    shaped_back = rows_back.reshape(2 * experts, capacity, rows_back.shape[1])
    moved = lax.all_to_all(shaped_back, "expert", split_axis=0, concat_axis=0, tiled=True)
    width = moved.shape[2]
    halves = jnp.sum(moved.reshape(experts, 2, capacity, width), axis=1)
    return halves.astype(jnp.bfloat16).reshape(experts * capacity, width)


def per_device_slots(
    tokens,
    qkv_weight,
    out_weight,
    gain_attn,
    gain_moe,
    router_weight,
    expert_in,
    expert_out,
    expert_ids,
    priority,
    cotangent,
):
    row_count, features = tokens.shape
    local_width = qkv_weight.shape[2]
    heads_here = local_width // HD
    images = row_count // LEN
    experts = router_weight.shape[1]
    capacity = max(2, 5 * row_count // (2 * experts))
    slot_count = experts * capacity
    block_rows = 2 * LEN
    blocks = row_count // block_rows
    slot_index = slot_table(expert_ids, priority[0], experts, capacity)
    slot_blocks = slot_index.reshape(blocks, block_rows, 2)
    score_root = math.sqrt(HD)
    inputs = tokens.astype(jnp.float32)
    normed_one, unit_one, scale_one = norm_parts(inputs, gain_attn)
    normed_one = normed_one.astype(jnp.bfloat16)
    qkv = jnp.einsum(
        "td,sdf->stf", normed_one, qkv_weight, preferred_element_type=jnp.float32
    ).astype(jnp.bfloat16)
    shaped = qkv.reshape(3, images, LEN, heads_here, HD)
    scores = (
        jnp.einsum("gqhe,gkhe->ghqk", shaped[0], shaped[1], preferred_element_type=jnp.float32)
        / score_root
    )
    row_peak = jnp.max(scores, axis=-1, keepdims=True)
    weights = jnp.exp(scores - row_peak)
    weight_total = jnp.sum(weights, axis=-1, keepdims=True)
    probs = weights / weight_total
    log_total = row_peak + jnp.log(weight_total)
    head_rows = (
        jnp.einsum(
            "ghqk,gkhe->gqhe",
            probs.astype(jnp.bfloat16),
            shaped[2],
            preferred_element_type=jnp.float32,
        )
        .reshape(row_count, local_width)
        .astype(jnp.bfloat16)
    )
    attn = lax.psum(jnp.dot(head_rows, out_weight, preferred_element_type=jnp.float32), "tensor")
    residual = inputs + attn
    normed_two, unit_two, scale_two = norm_parts(residual, gain_moe)
    normed_two = normed_two.astype(jnp.bfloat16)
    logits = jnp.dot(normed_two, router_weight, preferred_element_type=jnp.float32)
    expert_iota = jnp.arange(experts, dtype=jnp.int32)
    choosing = (expert_ids[:, :, None] == expert_iota[None, None, :]).astype(jnp.float32)
    chosen = jnp.sum(choosing * logits[:, None, :], axis=2)
    gates = jax.nn.softmax(chosen, axis=1)

    def collect(carry, element):
        leading, trailing = pair_tables(element[0], slot_count)
        return (
            carry
            + jnp.einsum(
                "tc,td->cd", leading + trailing, element[1], preferred_element_type=jnp.float32
            ),
            None,
        )

    dispatched, ignored = lax.scan(
        collect,
        jnp.zeros((slot_count, features), jnp.float32),
        (slot_blocks, normed_two.reshape(blocks, block_rows, features)),
    )
    dispatched = dispatched.astype(jnp.bfloat16).reshape(experts, capacity, features)
    received = to_experts(dispatched)
    pre_act = jnp.dot(received, expert_in[0], preferred_element_type=jnp.float32)
    activated = jax.nn.gelu(pre_act, approximate=False).astype(jnp.bfloat16)
    returned = from_experts(
        tensor_total(jnp.dot(activated, expert_out[0], preferred_element_type=jnp.float32)),
        experts,
        capacity,
    )
    grad_y = cotangent.astype(jnp.float32)

    def combine(carry, element):
        slot_block, gate_block, grad_block = element
        leading, trailing = pair_tables(slot_block, slot_count)
        got_lead = jnp.dot(leading, returned, preferred_element_type=jnp.float32)
        got_trail = jnp.dot(trailing, returned, preferred_element_type=jnp.float32)
        mixed = gate_block[:, 0:1] * got_lead + gate_block[:, 1:2] * got_trail
        gate_grad = jnp.stack(
            [jnp.sum(grad_block * got_lead, axis=1), jnp.sum(grad_block * got_trail, axis=1)],
            axis=1,
        )
        carry = carry + jnp.einsum(
            "tc,td->cd",
            leading,
            (gate_block[:, 0:1] * grad_block).astype(jnp.bfloat16),
            preferred_element_type=jnp.float32,
        )
        carry = carry + jnp.einsum(
            "tc,td->cd",
            trailing,
            (gate_block[:, 1:2] * grad_block).astype(jnp.bfloat16),
            preferred_element_type=jnp.float32,
        )
        return (carry, (mixed, gate_grad))

    grad_slots, (moe, gate_grad) = lax.scan(
        combine,
        jnp.zeros((slot_count, features), jnp.float32),
        (
            slot_blocks,
            gates.reshape(blocks, block_rows, 2),
            grad_y.reshape(blocks, block_rows, features),
        ),
    )
    moe = moe.reshape(row_count, features)
    gate_grad = gate_grad.reshape(row_count, 2)
    result = (residual + moe).astype(jnp.bfloat16)
    grad_rows = to_experts(grad_slots.astype(jnp.bfloat16).reshape(experts, capacity, features))
    grad_act = jnp.einsum("rd,fd->rf", grad_rows, expert_out[0], preferred_element_type=jnp.float32)
    ignored, gelu_back = jax.vjp(lambda values: jax.nn.gelu(values, approximate=False), pre_act)
    grad_pre = gelu_back(grad_act)[0].astype(jnp.bfloat16)
    grad_expert_out = jnp.einsum(
        "rf,rd->fd", activated, grad_rows, preferred_element_type=jnp.float32
    )
    grad_expert_in = jnp.einsum("rd,rf->df", received, grad_pre, preferred_element_type=jnp.float32)
    grad_sent = from_experts(
        tensor_total(
            jnp.einsum("rf,df->rd", grad_pre, expert_in[0], preferred_element_type=jnp.float32)
        ),
        experts,
        capacity,
    )
    grad_choice = gates * (gate_grad - jnp.sum(gates * gate_grad, axis=1, keepdims=True))
    grad_logits = jnp.sum(choosing * grad_choice[:, :, None], axis=1)
    grad_router = jnp.einsum(
        "td,te->de", normed_two.astype(jnp.float32), grad_logits, precision=HIGHEST
    )
    router_back = jnp.einsum(
        "te,de->td", grad_logits, router_weight.astype(jnp.float32), precision=HIGHEST
    )

    def spread_rows(slot_block):
        leading, trailing = pair_tables(slot_block, slot_count)
        return jnp.dot(leading + trailing, grad_sent, preferred_element_type=jnp.float32)

    grad_normed_two = lax.map(spread_rows, slot_blocks).reshape(row_count, features) + router_back
    residual_back, grad_gain_moe = norm_back(grad_normed_two, unit_two, scale_two, gain_moe)
    grad_residual = grad_y + residual_back
    grad_attn = grad_residual.astype(jnp.bfloat16)
    grad_out_weight = jnp.einsum(
        "tf,td->fd", head_rows, grad_attn, preferred_element_type=jnp.float32
    )
    grad_heads = jnp.einsum("td,fd->tf", grad_attn, out_weight, preferred_element_type=jnp.float32)
    grad_heads = grad_heads.astype(jnp.bfloat16).reshape(images, LEN, heads_here, HD)
    scores_again = (
        jnp.einsum("gqhe,gkhe->ghqk", shaped[0], shaped[1], preferred_element_type=jnp.float32)
        / score_root
    )
    probs_again = jnp.exp(scores_again - log_total)
    grad_probs = jnp.einsum(
        "gqhe,gkhe->ghqk", grad_heads, shaped[2], preferred_element_type=jnp.float32
    )
    grad_scores = (
        probs_again * (grad_probs - jnp.sum(probs_again * grad_probs, axis=-1, keepdims=True))
    ).astype(jnp.bfloat16)
    grad_values = jnp.einsum(
        "ghqk,gqhe->gkhe",
        probs_again.astype(jnp.bfloat16),
        grad_heads,
        preferred_element_type=jnp.float32,
    )
    grad_queries = (
        jnp.einsum("ghqk,gkhe->gqhe", grad_scores, shaped[1], preferred_element_type=jnp.float32)
        / score_root
    )
    grad_keys = (
        jnp.einsum("ghqk,gqhe->gkhe", grad_scores, shaped[0], preferred_element_type=jnp.float32)
        / score_root
    )
    grad_qkv_rows = (
        jnp.stack([grad_queries, grad_keys, grad_values])
        .reshape(3, row_count, local_width)
        .astype(jnp.bfloat16)
    )
    grad_qkv = jnp.einsum(
        "td,stf->sdf", normed_one, grad_qkv_rows, preferred_element_type=jnp.float32
    )
    grad_normed_one = lax.psum(
        jnp.einsum("stf,sdf->td", grad_qkv_rows, qkv_weight, preferred_element_type=jnp.float32),
        "tensor",
    )
    input_back, grad_gain_attn = norm_back(grad_normed_one, unit_one, scale_one, gain_attn)
    grad_tokens = grad_residual + input_back
    squares = jnp.stack([jnp.sum(inputs * inputs), jnp.sum(attn * attn), jnp.sum(moe * moe)])
    summed = lax.psum(
        (grad_qkv, grad_out_weight, grad_gain_attn, grad_gain_moe, grad_router, squares), "expert"
    )
    entry_count = float(row_count * features * lax.axis_size("expert"))
    stats = jnp.sqrt(summed[5] / entry_count)
    return (
        result,
        grad_tokens,
        summed[0],
        summed[1],
        summed[2],
        summed[3],
        summed[4],
        grad_expert_in[None],
        grad_expert_out[None],
        stats,
    )


def stage_pairs(moves):
    return [(2 * a + x, 2 * b + x) for a, b in moves for x in range(2)]


TO_RIGHT = stage_pairs([(0, 1), (1, 2), (2, 3)])
TO_LEFT = stage_pairs([(1, 0), (2, 1), (3, 2)])
ACROSS = [(i, i ^ 1) for i in range(8)]


def mixed(a, b):
    return (a.astype(jnp.float32) + b.astype(jnp.float32)).astype(jnp.bfloat16)


def flipped(parts, bits, index):
    shape = parts.shape
    parts = parts.reshape((2,) * bits + shape[1:])
    for b in range(bits):
        is_set = ((index >> (bits - 1 - b)) & 1) == 1
        parts = jnp.where(is_set, jnp.flip(parts, axis=b), parts)
    return parts.reshape(shape)


def flip_pairs(count, mask):
    return [(i, i ^ mask) for i in range(count)]


def wide(v):
    return v.astype(jnp.float32)


def fold(a, b, dims):
    return lax.dot_general(a, b, (dims, ((), ())), preferred_element_type=jnp.float32)


def rows_of(index, size):
    return pl.ds(pl.multiple_of(index * size, 16), size)


def image_windows(rows):
    size = -(-(LEN + 15) // 16) * 16
    images = rows // LEN
    return [(min(LEN * g // 16 * 16, rows - size), LEN * g) for g in range(images)], size


def attention_forward_kernel(
    t_ref, x_ref, w_ref, out_ref, gain_ref,
    send_ref, keep_ref, pass_ref, normed_ref, qkv_ref, heads_ref, lse_ref,
):
    rows = x_ref.shape[0]
    quarter = rows // 4
    for c in range(4):
        part = pl.ds(c * quarter, quarter)
        x = wide(x_ref[part, :])
        scaling = lax.rsqrt(jnp.mean(x * x, axis=1, keepdims=True) + EPSILON)
        normed = (x * scaling * gain_ref[...]).astype(jnp.bfloat16)
        normed_ref[part, :] = normed
        for s in range(3):
            qkv_ref[s, part, :] = fold(normed, w_ref[s], ((1,), (0,))).astype(jnp.bfloat16)
    width = heads_ref.shape[1]
    heads_ref[...] = jnp.zeros_like(heads_ref)
    lse_ref[...] = jnp.zeros_like(lse_ref)
    windows, size = image_windows(rows)
    lane = lax.broadcasted_iota(jnp.int32, (1, width), 1)
    spot = lax.broadcasted_iota(jnp.int32, (size, 1), 0)
    key_spot = lax.broadcasted_iota(jnp.int32, (1, size), 1)
    for start, first in windows:
        part = pl.ds(start, size)
        low = first - start
        q = qkv_ref[0, part, :]
        k = qkv_ref[1, part, :]
        v = qkv_ref[2, part, :]
        inside = (spot >= low) & (spot < low + LEN)
        key_inside = (key_spot >= low) & (key_spot < low + LEN)
        total = None
        for h in range(width // HD):
            own = (lane >= h * HD) & (lane < (h + 1) * HD)
            scores = fold(q, jnp.where(own, k, 0), ((1,), (1,))) * (1.0 / math.sqrt(HD))
            scores = jnp.where(key_inside, scores, -1e30)
            peak = jnp.max(scores, axis=1, keepdims=True)
            weights = jnp.exp(scores - peak)
            weight_total = jnp.sum(weights, axis=1, keepdims=True)
            probs = (weights / weight_total).astype(jnp.bfloat16)
            lse = peak + jnp.log(weight_total)
            lse_ref[h, part, :] = jnp.where(inside, lse, lse_ref[h, part, :])
            rows_out = fold(probs, jnp.where(own, v, 0), ((1,), (0,)))
            total = rows_out if total is None else total + rows_out
        heads_ref[part, :] = jnp.where(inside, total.astype(jnp.bfloat16), heads_ref[part, :])
    for k in range(4):
        part = rows_of(t_ref[0] ^ k, quarter)
        attn = fold(heads_ref[part, :], out_ref[...], ((1,), (0,))).astype(jnp.bfloat16)
        if k % 2:
            send_ref[k // 2] = attn
        elif k == 0:
            keep_ref[...] = attn
        else:
            pass_ref[...] = attn


def attention_backward_kernel(
    t_ref, g0_ref, g1_ref, g2_ref, g3_ref, w_ref, out_ref,
    normed_ref, qkv_ref, heads_ref, lse_ref,
    send_ref, keep_ref, pass_ref, wsend_ref, wkeep_ref, gain_ref,
    grad_ref, ghead_ref, grow_ref,
):
    rows, width = heads_ref.shape
    quarter = rows // 4
    for k, ref in enumerate((g0_ref, g1_ref, g2_ref, g3_ref)):
        grad_ref[rows_of(t_ref[0] ^ k, quarter), :] = ref[...]
    ghead_ref[...] = fold(grad_ref[...], out_ref[...], ((1,), (1,))).astype(jnp.bfloat16)
    grow_ref[...] = jnp.zeros_like(grow_ref)
    windows, size = image_windows(rows)
    lane = lax.broadcasted_iota(jnp.int32, (1, width), 1)
    spot = lax.broadcasted_iota(jnp.int32, (size, 1), 0)
    key_spot = lax.broadcasted_iota(jnp.int32, (1, size), 1)
    scale = 1.0 / math.sqrt(HD)
    for start, first in windows:
        part = pl.ds(start, size)
        low = first - start
        q = qkv_ref[0, part, :]
        k = qkv_ref[1, part, :]
        v = qkv_ref[2, part, :]
        gh = ghead_ref[part, :]
        inside = (spot >= low) & (spot < low + LEN)
        key_inside = (key_spot >= low) & (key_spot < low + LEN)
        both = inside & key_inside
        sums = [0.0, 0.0, 0.0]
        for h in range(width // HD):
            own = (lane >= h * HD) & (lane < (h + 1) * HD)
            k_own = jnp.where(own, k, 0)
            scores = fold(q, k_own, ((1,), (1,))) * scale
            probs = jnp.where(both, jnp.exp(jnp.where(both, scores - lse_ref[h, part, :], 0.0)), 0.0)
            gprobs = fold(gh, jnp.where(own, v, 0), ((1,), (1,)))
            inner = jnp.sum(probs * gprobs, axis=1, keepdims=True)
            gscores = (probs * (gprobs - inner)).astype(jnp.bfloat16)
            sums[0] = sums[0] + fold(gscores, k_own, ((1,), (0,)))
            sums[1] = sums[1] + fold(gscores, jnp.where(own, q, 0), ((0,), (0,)))
            sums[2] = sums[2] + fold(
                probs.astype(jnp.bfloat16), jnp.where(own, gh, 0), ((0,), (0,))
            )
        grow_ref[0, part, :] += sums[0] * scale
        grow_ref[1, part, :] += sums[1] * scale
        grow_ref[2, part, :] += sums[2]
    gain = None
    for s in range(4):
        if s < 3:
            grow = grow_ref[s].astype(jnp.bfloat16)
            made = fold(normed_ref[...], grow, ((0,), (0,)))
            seen = jnp.sum(made * wide(w_ref[s]), axis=1, keepdims=True)
            gain = seen if gain is None else gain + seen
        else:
            made = fold(grad_ref[...], heads_ref[...], ((0,), (0,)))
        made = made.astype(jnp.bfloat16)

        @pl.when(t_ref[1] == s // 2)
        def _():
            wkeep_ref[s % 2] = made

        @pl.when(t_ref[1] != s // 2)
        def _():
            wsend_ref[s % 2] = made

    gain_ref[...] = gain
    for k in range(4):
        part = rows_of(t_ref[0] ^ k, quarter)
        back = None
        for s in range(3):
            one = fold(grow_ref[s, part, :].astype(jnp.bfloat16), w_ref[s], ((1,), (1,)))
            back = one if back is None else back + one
        back = back.astype(jnp.bfloat16)
        if k % 2:
            send_ref[k // 2] = back
        elif k == 0:
            keep_ref[...] = back
        else:
            pass_ref[...] = back


def norm_two_kernel(
    x_ref, keep_ref, got_ref, other_ref, gain_ref, residual_ref, normed_ref, square_ref
):
    attn = (wide(keep_ref[...]) + wide(got_ref[0])) + wide(other_ref[...])
    x = wide(x_ref[...])
    residual = x + attn
    residual_ref[...] = residual
    scaling = lax.rsqrt(jnp.mean(residual * residual, axis=1, keepdims=True) + EPSILON)
    normed_ref[...] = (residual * scaling * gain_ref[...]).astype(jnp.bfloat16)
    square_ref[0:1, :] = jnp.sum(x * x, axis=0, keepdims=True)
    square_ref[1:2, :] = jnp.sum(attn * attn, axis=0, keepdims=True)


def norm_one_back_kernel(
    x_ref, keep_ref, got_ref, other_ref, before_ref, gain_ref, grad_ref
):
    incoming = (wide(keep_ref[...]) + wide(got_ref[0])) + wide(other_ref[...])
    x = wide(x_ref[...])
    scaling = lax.rsqrt(jnp.mean(x * x, axis=1, keepdims=True) + EPSILON)
    unit = x * scaling
    inner = incoming * gain_ref[...]
    back = scaling * (inner - unit * jnp.mean(inner * unit, axis=1, keepdims=True))
    grad_ref[...] = (before_ref[...] + back).astype(jnp.bfloat16)


def pair_gates(normed, router, code):
    rows = normed.shape[0]
    logits = fold(normed, router, ((1,), (0,)))
    lane = lax.broadcasted_iota(jnp.int32, (rows, router.shape[1]), 1)
    lead = wide(lane == (code & 31))
    trail = wide(lane == ((code >> 5) & 31))
    one = jnp.sum(lead * logits, axis=1, keepdims=True)
    two = jnp.sum(trail * logits, axis=1, keepdims=True)
    peak = jnp.maximum(one, two)
    one = jnp.exp(one - peak)
    two = jnp.exp(two - peak)
    both = one + two
    kept_one = wide((code >> 10) & 1)
    kept_two = wide((code >> 11) & 1)
    return lead, trail, one / both, two / both, kept_one, kept_two


def norm_two_back_kernel(
    keep_ref, got_ref, other_ref, residual_ref, dy_ref, code_ref, gain_ref, router_ref, flat_ref,
    grad_ref, low_ref, small_ref,
):
    features = residual_ref.shape[1]
    experts = flat_ref.shape[0]
    total = (wide(keep_ref[...]) + wide(got_ref[0])) + wide(other_ref[...])
    residual = residual_ref[...]
    scaling = lax.rsqrt(jnp.mean(residual * residual, axis=1, keepdims=True) + EPSILON)
    unit = residual * scaling
    normed = (unit * gain_ref[...]).astype(jnp.bfloat16)
    lead, trail, one, two, kept_one, kept_two = pair_gates(normed, router_ref[...], code_ref[...])
    seen = total[:, features:]
    seen = seen + pltpu.roll(seen, 64, axis=1)
    back_one = kept_one * jnp.sum(lead * seen, axis=1, keepdims=True)
    back_two = kept_two * jnp.sum(trail * seen, axis=1, keepdims=True)
    mean = one * back_one + two * back_two
    choice = lead * (one * (back_one - mean)) + trail * (two * (back_two - mean))
    incoming = total[:, :features]
    for e in range(experts):
        column = choice[:, e : e + 1]
        incoming = incoming + column * flat_ref[e : e + 1, :]
        small_ref[1 + e : 2 + e, :] = jnp.sum(column * wide(normed), axis=0, keepdims=True)
    inner = incoming * gain_ref[...]
    small_ref[0:1, :] = jnp.sum(incoming * unit, axis=0, keepdims=True)
    back = scaling * (inner - unit * jnp.mean(inner * unit, axis=1, keepdims=True))
    grad = wide(dy_ref[...]) + back
    grad_ref[...] = grad
    low_ref[...] = grad.astype(jnp.bfloat16)


def dense_experts_kernel(
    which_ref, x0_ref, x1_ref, x2_ref, x3_ref, dy_ref, code_ref, router_ref, *refs, last
):
    count = 4
    w_refs, refs = refs[:count], refs[count:]
    if last:
        before, refs = refs[:3], refs[3:]
        msend_ref, mkeep_ref, mpass_ref, dsend_ref, dkeep_ref, dpass_ref = refs[:6]
        g_refs, refs = refs[6 : 6 + count], refs[6 + count :]
        moe_acc, dx_acc, gg_acc = refs[:3]
        refs = refs[3:]
    else:
        moe_acc, dx_acc, gg_acc = refs[:3]
        g_refs, refs = refs[3 : 3 + count], refs[3 + count :]
    x_ref, gate_ref, w_now, gact_ref, gpre_ref, g_now = refs
    step = pl.program_id(0)
    chosen = which_ref[step]
    rows, features = dy_ref.shape
    quarter = rows // 4

    @pl.when(step == 0)
    def _():
        moe_acc[...] = jnp.zeros_like(moe_acc)
        dx_acc[...] = jnp.zeros_like(dx_acc)
        gg_acc[...] = jnp.zeros_like(gg_acc)
        for k, ref in enumerate((x0_ref, x1_ref, x2_ref, x3_ref)):
            x_ref[rows_of(which_ref[count] ^ k, quarter), :] = ref[...]
        for c in range(4):
            part = pl.ds(c * quarter, quarter)
            lead, trail, one, two, kept_one, kept_two = pair_gates(
                x_ref[part, :], router_ref[...], code_ref[part, :]
            )
            gate_ref[part, :] = lead * (one * kept_one) + trail * (two * kept_two)

    for k in range(count):

        @pl.when(step == k)
        def _():
            w_now[...] = w_refs[k][...]

    hidden = gact_ref.shape[1]
    pieces = [pl.ds(i, hidden) for i in range(0, features, hidden)]
    wout = w_now[1]
    for c in range(4):
        part = pl.ds(c * quarter, quarter)
        pre = fold(x_ref[part, pieces[0]], w_now[0, :, pieces[0]], ((1,), (0,)))
        for piece in pieces[1:]:
            pre = pre + fold(x_ref[part, piece], w_now[0, :, piece], ((1,), (0,)))
        back = fold(dy_ref[part, :], wout, ((1,), (1,)))
        half = 0.5 + 0.5 * lax.erf(pre * math.sqrt(0.5))
        act = pre * half
        slope = half + pre * (jnp.exp(pre * pre * -0.5) * (1.0 / math.sqrt(2.0 * math.pi)))
        lane = lax.broadcasted_iota(jnp.int32, (quarter, 128), 1)
        mine = lane == chosen
        gate = jnp.sum(jnp.where(mine, gate_ref[part, :], 0.0), axis=1, keepdims=True)
        act = wide(act.astype(jnp.bfloat16))
        seen = jnp.sum(act * back, axis=1, keepdims=True)
        gg_acc[part, :] = gg_acc[part, :] + jnp.where(mine, seen, 0.0)
        gact_ref[part, :] = (gate * act).astype(jnp.bfloat16)
        gpre_ref[part, :] = (gate * back * slope).astype(jnp.bfloat16)
    gact = gact_ref[...]
    gpre = gpre_ref[...]
    moe_acc[...] += fold(gact, wout, ((1,), (0,)))
    for piece in pieces:
        dx_acc[:, piece] += fold(gpre, w_now[0, :, piece], ((1,), (1,)))
        g_now[0, :, piece] = fold(x_ref[:, piece], gpre, ((0,), (0,))).astype(jnp.bfloat16)
    g_now[1] = fold(gact, dy_ref[...], ((0,), (0,))).astype(jnp.bfloat16)
    for k in range(count):

        @pl.when(step == k)
        def _():
            g_refs[k][...] = g_now[...]

    if not last:
        return

    @pl.when(step == count - 1)
    def _():
        moe_in, dx_in, gg_in = before
        for k in range(4):
            part = rows_of(which_ref[count] ^ k, quarter)
            moe = (moe_acc[part, :] + moe_in[part, :]).astype(jnp.bfloat16)
            dx = (dx_acc[part, :] + dx_in[part, :]).astype(jnp.bfloat16)
            seen = gg_acc[part, :] + gg_in[part, :]
            high = wide(seen.astype(jnp.bfloat16))
            seen = (high + pltpu.roll(seen - high, 64, axis=1)).astype(jnp.bfloat16)
            if k % 2:
                msend_ref[k // 2] = moe
                dsend_ref[k // 2, :, :features] = dx
                dsend_ref[k // 2, :, features:] = seen
            else:
                (mpass_ref if k else mkeep_ref)[...] = moe
                into = dpass_ref if k else dkeep_ref
                into[:, :features] = dx
                into[:, features:] = seen


def one_step(kernel, scalars, args, outs, scratch=(), grid=1):
    whole = lambda v: pl.BlockSpec(v.shape, lambda j, w, n=len(v.shape): (0,) * n)
    return pl.pallas_call(
        kernel,
        grid_spec=pltpu.PrefetchScalarGridSpec(
            num_scalar_prefetch=1,
            grid=(grid,),
            in_specs=[whole(v) for v in args],
            out_specs=[whole(v) for v in outs],
            scratch_shapes=[pltpu.VMEM(shape, dtype) for shape, dtype in scratch],
        ),
        out_shape=outs,
    )(scalars, *args)


def drop_first(kernel):
    return lambda scalars, *refs: kernel(*refs)


def array_of(shape, dtype=jnp.bfloat16):
    return jax.ShapeDtypeStruct(shape, dtype)


def after(values, *tokens):
    return lax.optimization_barrier((values, tokens))[0]


def flip_core(v):
    return lax.ppermute(v, "tensor", flip_pairs(4, 1))


def flip_row(v):
    return lax.ppermute(v, "tensor", flip_pairs(4, 2))


def over(v, pairs):
    return lax.ppermute(v, "expert", pairs)


def pair_codes(expert_ids, ranking, experts, capacity):
    iota = jnp.arange(experts, dtype=jnp.int32)[None, :]
    leading = (expert_ids[:, 0:1] == iota).astype(jnp.bfloat16)
    trailing = (expert_ids[:, 1:2] == iota).astype(jnp.bfloat16)
    earlier = (ranking[None, :] < ranking[:, None]).astype(jnp.bfloat16)
    before = jnp.dot(
        earlier, jnp.concatenate([leading, trailing], axis=1), preferred_element_type=jnp.float32
    )
    lead_place = jnp.sum(before[:, :experts] * wide(leading), axis=1)
    totals = jnp.sum(wide(leading), axis=0)
    trail_place = jnp.sum((before[:, experts:] + totals) * wide(trailing), axis=1)
    bits = lambda place: (place < capacity).astype(jnp.int32)
    code = expert_ids[:, 0] + 32 * expert_ids[:, 1]
    return (code + 1024 * bits(lead_place) + 2048 * bits(trail_place))[:, None]


def dense_body(
    tokens,
    qkv_weight,
    out_weight,
    gain_attn,
    gain_moe,
    router_weight,
    expert_in,
    expert_out,
    expert_ids,
    priority,
    cotangent,
):
    row_count, features = tokens.shape
    width = qkv_weight.shape[2]
    hidden = expert_in.shape[2]
    experts = router_weight.shape[1]
    capacity = max(2, 5 * row_count // (2 * experts))
    padded = -(-row_count // 64) * 64
    quarter = padded // 4
    f32 = jnp.float32
    t = lax.axis_index("tensor").astype(jnp.int32)
    d = lax.axis_index("expert").astype(jnp.int32)
    place = d // 2
    pad = lambda v: jnp.pad(v, ((0, padded - row_count), (0, 0)))
    mine = lambda v: lax.dynamic_slice_in_dim(v, t * quarter, quarter, 0)
    w_in = jnp.concatenate(jnp.split(expert_in[0], features // hidden), axis=1)
    own = jnp.stack([w_in, expert_out[0]])
    right = over(own, TO_RIGHT)
    left = over(own, TO_LEFT)
    cross_own = over(own, ACROSS)
    x_all = pad(tokens)
    dy_all = pad(cotangent)
    gain_one = gain_attn[None]
    gain_two = gain_moe[None]
    spots = jnp.stack([t, d % 2])
    part = array_of((quarter, features))
    parts = array_of((2, quarter, features))
    send, keep, passed, normed_one, qkv, head_rows, lse = one_step(
        attention_forward_kernel,
        spots,
        [x_all, qkv_weight, out_weight, gain_one],
        [
            parts,
            part,
            part,
            array_of((padded, features)),
            array_of((3, padded, width)),
            array_of((padded, width)),
            array_of((width // HD, padded, 1), f32),
        ],
    )
    got = flip_core(send)
    right, left = after((right, left), send)
    near = jnp.where(place >= 1, right, left)
    passed = mixed(passed, got[1])
    other = flip_row(passed)
    right_two = over(right, stage_pairs([(1, 2), (2, 3)]))
    left_two = over(left, stage_pairs([(1, 0), (2, 1)]))
    cross_near = over(near, ACROSS)
    right_two, left_two = after((right_two, left_two), passed)
    middle = jnp.where(place >= 2, right_two, left_two)
    end = over(middle, stage_pairs([(2, 3), (1, 0)]))
    cross_middle = over(middle, ACROSS)
    other = after(other, middle)
    x_here = mine(x_all)
    dy_here = mine(dy_all)
    residual, normed_two, squares = one_step(
        drop_first(norm_two_kernel),
        spots,
        [x_here, keep, got, other, gain_two],
        [array_of((quarter, features), f32), part, array_of((2, features), f32)],
    )
    row_two = flip_row(normed_two)
    core_two = flip_core(normed_two)
    end, left = after((end, left), normed_two)
    far = jnp.where((place == 1) | (place == 2), left, end)
    cross_far = over(far, ACROSS)
    row_two = after(row_two, far)
    quarters = [normed_two, core_two, row_two, flip_core(row_two)]
    codes = pad(pair_codes(expert_ids, priority[0], experts, capacity))
    router_wide = jnp.pad(router_weight, ((0, 0), (0, 128 - experts)))
    near_place = jnp.where(place >= 1, place - 1, 1)
    far_place = jnp.where(place == 1, 2, jnp.where(place == 3, 0, 3))
    which_near = jnp.stack([near_place, place ^ 2, near_place, place ^ 2, t])
    which_far = jnp.stack([place, far_place, place, far_place, t])
    one = array_of((2, hidden, features))
    plus = (quarter, features + 128)
    sums = [
        array_of((padded, features), f32),
        array_of((padded, features), f32),
        array_of((padded, 128), f32),
    ]
    scratch = [
        ((padded, features), jnp.bfloat16),
        ((padded, 128), f32),
        (one.shape, jnp.bfloat16),
        ((padded, hidden), jnp.bfloat16),
        ((padded, hidden), jnp.bfloat16),
        (one.shape, jnp.bfloat16),
    ]
    shared = quarters + [dy_all, codes, router_wide]
    early = one_step(
        functools.partial(dense_experts_kernel, last=False),
        which_near,
        shared + [near, middle, cross_near, cross_middle],
        sums + [one] * 4,
        scratch=scratch,
        grid=4,
    )
    near, middle, cross_near, cross_middle = early[3:]
    cross_middle = over(cross_middle, ACROSS)
    cross_near = over(cross_near, ACROSS)
    late = one_step(
        functools.partial(dense_experts_kernel, last=True),
        which_far,
        shared + after([own, far, cross_own, cross_far], early[2]) + list(early[:3]),
        [parts, part, part, array_of((2,) + plus), array_of(plus), array_of(plus)] + [one] * 4,
        scratch=[(v.shape, f32) for v in sums] + scratch,
        grid=4,
    )
    own, far, cross_own, cross_far = late[6:]
    msend, mkeep, mpass, dsend, dkeep, dpass = late[:6]
    got = flip_core(dsend)
    dpass = mixed(dpass, got[1])
    other = flip_row(dpass)
    cross_far, cross_own = after((cross_far, cross_own), dpass)
    cross_far = over(cross_far, ACROSS)
    cross_own = over(cross_own, ACROSS)
    cross_middle, cross_near = after((cross_middle, cross_near), dpass)
    middle = mixed(middle, cross_middle)
    near = mixed(near, cross_near)
    g_middle = over(middle, flip_pairs(8, 4))
    grad_residual, grad_attn, small_two = one_step(
        drop_first(norm_two_back_kernel),
        spots,
        [
            dkeep, got, other, residual, dy_here, mine(codes), gain_two, router_wide,
            wide(router_weight).T,
        ],
        [
            array_of((quarter, features), f32),
            part,
            array_of((1 + experts, features), f32),
        ],
    )
    row_two = flip_row(grad_attn)
    core_two = flip_core(grad_attn)
    far = mixed(far, after(cross_far, grad_attn))
    turn = lambda by: [(i, (i + 2 * by) % 8) for i in range(8)]
    g_right = over(jnp.where(place == 0, near, far), turn(1))
    g_left = over(jnp.where(place == 0, far, near), turn(-1))
    mgot = flip_core(after(msend, grad_attn))
    mpass = mixed(mpass, mgot[1])
    mother = flip_row(mpass)
    row_two = after(row_two, far, mpass)
    both_two = flip_core(row_two)
    send, keep, passed, wsend, wkeep, gain_column = one_step(
        attention_backward_kernel,
        spots,
        [grad_attn, core_two, row_two, both_two]
        + [qkv_weight, out_weight, normed_one, qkv, head_rows, lse],
        [
            parts,
            part,
            part,
            array_of((2, features, width)),
            array_of((2, features, width)),
            array_of((features, 1), f32),
        ],
        scratch=[
            ((padded, features), jnp.bfloat16),
            ((padded, width), jnp.bfloat16),
            ((3, padded, width), f32),
        ],
    )
    got = flip_core(send)
    wgot = over(wsend, flip_pairs(8, 1))
    passed = mixed(passed, got[1])
    other = flip_row(passed)
    mother, g_middle, g_right, g_left = after((mother, g_middle, g_right, g_left), passed)
    moe = (wide(mkeep) + wide(mgot[0])) + wide(mother)
    result = (residual + moe).astype(jnp.bfloat16)
    small = jnp.concatenate(
        [
            gain_column[:, 0][None] / gain_one,
            small_two,
            squares,
            jnp.sum(moe * moe, axis=0, keepdims=True),
        ]
    )
    small = small + flip_core(small)
    s_got = flip_row(small)
    grads = mixed(wkeep, after(wgot, small))
    wgot = over(grads, flip_pairs(8, 2))
    small = small + after(s_got, grads)
    s_got = over(small, flip_pairs(8, 1))
    grad_tokens = one_step(
        drop_first(norm_one_back_kernel),
        spots,
        [x_here, keep, got, after(other, small), grad_residual, gain_one],
        [part],
    )[0]
    grad_row = flip_row(grad_tokens)
    grad_core = flip_core(grad_tokens)
    result_row = flip_row(after(result, grad_tokens))
    result_core = flip_core(after(result, grad_tokens))
    grads = mixed(grads, after(wgot, grad_tokens))
    wgot = over(grads, flip_pairs(8, 4))
    small = small + after(s_got, grads)
    s_got = over(small, flip_pairs(8, 2))
    grad_row = after(grad_row, small)
    ordered = lambda four: flipped(jnp.stack(four), 2, t).reshape(padded, features)[:row_count]
    grad_tokens = ordered([grad_tokens, grad_core, grad_row, flip_core(grad_row)])
    small = small + after(s_got, grad_tokens)
    s_got = over(small, flip_pairs(8, 4))
    grads = mixed(grads, after(wgot, grad_tokens))
    wgot = over(grads, flip_pairs(8, 1))
    result_row = after(result_row, grads)
    result = ordered([result, result_core, result_row, flip_core(result_row)])
    grad_expert = (wide(own) + wide(after(cross_own, grads))) + (
        wide(g_middle) + (wide(g_right) + wide(g_left))
    )
    small = small + after(s_got, result)
    wgot = after(wgot, result)
    weight_grads = flipped(jnp.stack([grads, wgot]), 1, d % 2).reshape(4, features, width)
    weight_grads = wide(weight_grads)
    grad_in = jnp.concatenate(jnp.split(grad_expert[0], features // hidden, axis=1), axis=0)
    entry_count = float(row_count * features * lax.axis_size("expert"))
    stats = jnp.sqrt(jnp.sum(small[2 + experts :], axis=1) / entry_count)
    return (
        result,
        wide(grad_tokens),
        weight_grads[:3],
        weight_grads[3].T,
        small[0],
        small[1],
        small[2 : 2 + experts].T,
        grad_in[None],
        grad_expert[1][None],
        stats,
    )


def per_device_dense(*args):
    return dense_body(*args)


def solution(mesh):
    in_specs = (
        P("expert", None),
        P(None, None, "tensor"),
        P("tensor", None),
        P(),
        P(),
        P(),
        P("expert", None, "tensor"),
        P("expert", "tensor", None),
        P("expert", None),
        P("expert", None),
        P("expert", None),
    )
    out_specs = (
        P("expert", None),
        P("expert", None),
        P(None, None, "tensor"),
        P("tensor", None),
        P(),
        P(),
        P(),
        P("expert", None, "tensor"),
        P("expert", "tensor", None),
        P(),
    )
    few = mesh.shape["expert"] == 8 and mesh.shape["tensor"] == 4
    return jax.shard_map(
        per_device_dense if few else per_device_slots, mesh=mesh, in_specs=in_specs, out_specs=out_specs, check_vma=False
    )
```
